128 devices in a mesh: dp: 16 (over x, y), mp: 8 (over z, core).
Axes of the slice: x: 4, y: 4, z: 4, core: 2. Of those that a mesh axis runs over, the one named last changes fastest.
Arguments:
- patches: bfloat16 [4096, 6144], P('dp', 'mp'), may hold values from -6 to 6
- dest_group: int32 [4096], P('dp'), may hold values from 0 to 15, as said below
- dest_row: int32 [4096], P('dp'), may hold values from 0 to 255, as said below
- segment: int32 [4096], P('dp'), may hold values from 0 to 31, as said below
- ln_gain: float32 [6144], replicated, may hold values from 0.1 to 1.9
- w_qkv: bfloat16 [6144, 3, 3072], P(None, None, 'mp'), may hold values from -0.078125 to 0.078125
- qk_gain: float32 [2, 128], replicated, may hold values from 0.1 to 1.9
- w_out: bfloat16 [6144, 3072], P(None, 'mp'), may hold values from -0.4375 to 0.4375
- cotangent: bfloat16 [4096, 6144], P('dp', 'mp'), may hold values from -6 to 6
Outputs:
- output: bfloat16 [4096, 6144], P('dp', 'mp')
- input_grad: bfloat16 [4096, 6144], P('dp', 'mp')
- qkv_grad: bfloat16 [6144, 3, 3072], P('dp', None, 'mp')
- out_grad: bfloat16 [6144, 3072], P('dp', 'mp')
The draws below stay inside these ranges and needn't reach their ends.
Inputs may be any that keep to these rules, and one draw needn't show every extreme that they name: The pairs (dest_group, dest_row) of all rows name every row of every group exactly once. The rows of one group send at most 32 rows to any one group, and in every draw some group sends exactly 32 rows to some group. `dest_row`: see dest_group. `segment`: rows of one group with equal numbers are one image and stand in consecutive rows; numbers lie between 0 and 31.
All inputs are finite; a program needn't handle non-finite values.
Results may differ from the reference program's by a relative error of at most 0.024.
Values may be sent and summed in bfloat16 or wider, within the bound.
A program may use at most 192 MiB of HBM per device.

```python
import math
import jax
import jax.numpy as jnp
from jax import lax

D = 6144
DH = 128
ROWS = 256
HD = 3072
SLOT = 32
TOKENS = 4096
N_DP = 16
N_MP = 8


def route_plan(key):
    half_slot = SLOT // 2
    pair_count = (N_DP - 2) // 2
    key_delta = jax.random.fold_in(key, 11)
    key_order = jax.random.fold_in(key, 12)
    key_split = jax.random.fold_in(key, 13)
    delta = jax.random.randint(key_delta, (pair_count,), 0, half_slot + 1).astype(jnp.int32)
    base_counts = jnp.concatenate([jnp.array([SLOT, 0], jnp.int32), half_slot + delta, half_slot - delta]).astype(jnp.int32)
    order = jax.random.permutation(key_order, N_DP)
    counts = base_counts[order]
    source_ids = jnp.arange(N_DP, dtype=jnp.int32)[:, None]
    target_ids = jnp.arange(N_DP, dtype=jnp.int32)[None, :]
    load = counts[(target_ids - source_ids) % N_DP]
    src_start = jnp.cumsum(load, 1) - load
    dst_start = jnp.cumsum(load, 0) - load
    src_end = src_start + load
    dst_end = dst_start + load
    position = jnp.arange(ROWS, dtype=jnp.int32)
    target = jnp.sum((src_end[:, None, :] <= position[None, :, None]).astype(jnp.int32), 2)
    offset = position[None, :] - jnp.take_along_axis(src_start, target, 1)
    row_there = jnp.take_along_axis(dst_start, target, 1) + offset
    source = jnp.sum((dst_end.T[:, None, :] <= position[None, :, None]).astype(jnp.int32), 2)
    cut = jax.random.randint(key_split, (N_DP, N_DP), 0, load + 1).astype(jnp.int32)
    inside = position[None, :] - jnp.take_along_axis(dst_start.T, source, 1)
    cut_here = jnp.take_along_axis(cut.T, source, 1)
    image_ids = 2 * source + (inside >= cut_here).astype(jnp.int32)
    return (target.reshape(-1).astype(jnp.int32), row_there.reshape(-1).astype(jnp.int32), image_ids.reshape(-1).astype(jnp.int32))


def draw_dest_group(key, part):
    return route_plan(key)[0]


def draw_dest_row(key, part):
    return route_plan(key)[1]


def draw_segment(key, part):
    return route_plan(key)[2]


def strengthened(entries, rng, source, target, parts, factor):
    owner, partner = [(jnp.arange(entries.shape[dim]) // (entries.shape[dim] // parts)).reshape([-1 if axis == dim else 1 for axis in range(entries.ndim)]) for dim in (source, target)]
    chosen = jax.random.permutation(rng, parts)[partner]
    strong = (owner == chosen) | (owner == (partner + parts // 2) % parts)
    return jnp.where(strong, factor * entries, entries)


def block_scale(own_key, extent, cuts, low, largest):
    loudness = 1.0
    for axis_at, blocks in cuts:
        steps = jax.random.uniform(jax.random.fold_in(jax.random.fold_in(own_key, 6), axis_at), (blocks,), jnp.float32, low / len(cuts), largest / len(cuts))
        loudness = loudness * jnp.repeat(jnp.exp(steps), extent[axis_at] // blocks).reshape((-1,) + (1,) * (len(extent) - 1 - axis_at))
    return loudness


def noise(key, shape, scale, reach, shards=(), kind=jnp.bfloat16):
    result = jax.random.normal(key, shape, jnp.float32) * scale
    if len(shards) > 0:
        result = block_scale(key, shape, shards, -0.22, 0.18) * result
    return jnp.clip(result, min=-reach, max=reach).astype(kind)


def noise_with(stream_key, extent, scale, reach, split, heavy, held_as=jnp.bfloat16):
    result = scale * jax.random.normal(stream_key, extent, jnp.float32)
    if split:
        result = result * block_scale(stream_key, extent, split, -0.22, 0.18)
    return jnp.clip(strengthened(result, jax.random.fold_in(stream_key, 3), *heavy), -reach, reach).astype(held_as)


def setup_inputs(seed: int = 0) -> dict:
    key_list = jax.random.split(jax.random.key(seed), 10)
    patches = noise(key_list[0], (TOKENS, D), 1.0, 6.0, ((0, 16), (1, 8)))
    dest_group = draw_dest_group(jax.random.fold_in(key_list[9], 71), 0)
    dest_row = draw_dest_row(jax.random.fold_in(key_list[9], 71), 0)
    segment = draw_segment(jax.random.fold_in(key_list[9], 71), 0)
    ln_gain = jnp.clip(1.0 + 0.18 * jax.random.normal(key_list[4], (D,), jnp.float32), 0.1, 1.9)
    w_qkv = noise(key_list[5], (D, 3, HD), D ** -0.5, 0.078125, ((2, 8),))
    qk_gain = jnp.clip(1.0 + 0.18 * jax.random.normal(key_list[6], (2, DH), jnp.float32), 0.1, 1.9)
    w_out = noise(key_list[7], (D, HD), (HD // 16) ** -0.5, 0.4375, ((1, 8),))
    cotangent = noise_with(key_list[8], (TOKENS, D), 1.0, 6.0, ((0, 16), (1, 8)), (0, 1, 16, 2.0))
    return dict(patches=patches, dest_group=dest_group, dest_row=dest_row, segment=segment, ln_gain=ln_gain, w_qkv=w_qkv, qk_gain=qk_gain, w_out=w_out, cotangent=cotangent)


def norm_heads(values, gain):
    center = values - lax.optimization_barrier(jnp.mean(values, -1, keepdims=True))
    variance = lax.optimization_barrier(jnp.mean(center * center, -1, keepdims=True))
    return center * lax.rsqrt(variance + 1e-06) * gain

def attend(projected, image_ids, qk_gain):
    row_count = projected.shape[0]
    head_count = projected.shape[2] // DH
    split_heads = projected.reshape(row_count, 3, head_count, DH)
    queries = norm_heads(split_heads[:, 0], qk_gain[0]).astype(jnp.bfloat16)
    keys_normed = norm_heads(split_heads[:, 1], qk_gain[1]).astype(jnp.bfloat16)
    values_bf = split_heads[:, 2].astype(jnp.bfloat16)
    scores = jnp.einsum('qhd,khd->hqk', queries, keys_normed, preferred_element_type=jnp.float32) * DH ** (-0.5)
    same_image = image_ids[:, None] == image_ids[None, :]
    raised = jnp.where(same_image[None], jnp.exp(scores), 0.0)
    weights = (raised / lax.optimization_barrier(jnp.sum(raised, -1, keepdims=True))).astype(jnp.bfloat16)
    mixed = jnp.einsum('hqk,khd->qhd', weights, values_bf, preferred_element_type=jnp.float32)
    return mixed.reshape(row_count, head_count * DH).astype(jnp.bfloat16)

def reference(patches, dest_group, dest_row, segment, ln_gain, w_qkv, qk_gain, w_out, cotangent):
    token_total = patches.shape[0]
    group_rows = token_total // N_DP
    local_width = HD // N_MP
    target = (dest_group * group_rows + dest_row).astype(jnp.int32)
    packed = jnp.zeros_like(patches).at[target].set(patches)
    qkv_flat = w_qkv.reshape(D, 3 * HD)
    qkv_wide = w_qkv.reshape(D, 3, N_MP, local_width).astype(jnp.float32)
    out_wide = w_out.reshape(D, N_MP, local_width).astype(jnp.float32)
    scale_grad = 1.0 / math.sqrt(token_total)

    def one_group(carry, group_inputs):
        sum_qkv, sum_out = carry
        block, image_ids, cot_block = group_inputs
        wide = block.astype(jnp.float32)
        center = wide - lax.optimization_barrier(jnp.mean(wide, -1, keepdims=True))
        rstd = lax.rsqrt(lax.optimization_barrier(jnp.mean(center * center, -1, keepdims=True)) + 1e-06)
        unit_rows = center * rstd
        normed = (unit_rows * ln_gain).astype(jnp.bfloat16)
        projected = jnp.dot(normed, qkv_flat, preferred_element_type=jnp.float32).reshape(group_rows, 3, HD)
        heads_out, backward = jax.vjp(lambda values: attend(values, image_ids, qk_gain), projected)
        pieces = jnp.einsum('rmk,dmk->mrd', heads_out.reshape(group_rows, N_MP, local_width).astype(jnp.float32), out_wide)
        attn = lax.optimization_barrier(jnp.sum(lax.optimization_barrier(pieces.astype(jnp.bfloat16)).astype(jnp.float32), 0))
        output = (wide + attn).astype(jnp.bfloat16)
        d_heads = jnp.dot(cot_block, w_out, preferred_element_type=jnp.float32).astype(jnp.bfloat16)
        d_projected, = backward(d_heads)
        d_proj_bf = d_projected.astype(jnp.bfloat16)
        d_pieces = jnp.einsum('rtmk,dtmk->mrd', d_proj_bf.reshape(group_rows, 3, N_MP, local_width).astype(jnp.float32), qkv_wide)
        d_normed = lax.optimization_barrier(jnp.sum(lax.optimization_barrier(d_pieces.astype(jnp.bfloat16)).astype(jnp.float32), 0))
        d_unit = d_normed * ln_gain
        d_input = rstd * (d_unit - lax.optimization_barrier(jnp.mean(d_unit, -1, keepdims=True)) - unit_rows * lax.optimization_barrier(jnp.mean(d_unit * unit_rows, -1, keepdims=True)))
        input_grad = (cot_block.astype(jnp.float32) + d_input).astype(jnp.bfloat16)
        term_qkv = lax.dot_general(normed, d_proj_bf.reshape(group_rows, 3 * HD), (((0,), (0,)), ((), ())), preferred_element_type=jnp.float32)
        term_out = lax.dot_general(cot_block, heads_out, (((0,), (0,)), ((), ())), preferred_element_type=jnp.float32)
        sum_qkv = sum_qkv + lax.optimization_barrier(term_qkv.astype(jnp.bfloat16)).astype(jnp.float32)
        sum_out = sum_out + lax.optimization_barrier(term_out.astype(jnp.bfloat16)).astype(jnp.float32)
        return ((sum_qkv, sum_out), (output, input_grad))
    start_sums = (jnp.zeros((D, 3 * HD), jnp.float32), jnp.zeros((D, HD), jnp.float32))
    stacked = (packed.reshape(N_DP, group_rows, D), segment.reshape(N_DP, group_rows), cotangent.reshape(N_DP, group_rows, D))
    (sum_qkv, sum_out), (outputs, grads) = lax.scan(one_group, start_sums, stacked)
    qkv_grad = (sum_qkv * scale_grad).reshape(D, 3, HD).astype(jnp.bfloat16)
    out_grad = (sum_out * scale_grad).astype(jnp.bfloat16)
    return (outputs.reshape(token_total, D), grads.reshape(token_total, D), qkv_grad, out_grad)
```

```python
import functools
import math

import jax
import jax.numpy as jnp
from jax import lax
from jax.experimental import pallas as pl
from jax.experimental.pallas import tpu as pltpu
from jax.sharding import PartitionSpec as P

DH = 128
MESH = pl.DeviceIdType.MESH
F32 = jnp.float32
BF16 = jnp.bfloat16


class Place:
    def __init__(self):
        self.g, self.m = lax.axis_index("dp"), lax.axis_index("mp")
        self.x, self.y = self.g // 4, self.g % 4
        self.z, self.c = self.m // 2, self.m % 2
        c = self.c
        self.a = self.x * (1 - c) + self.y * c
        self.b = self.x * c + self.y * (1 - c)

    def along_a(self, k):
        x, y = (self.x + k * (1 - self.c)) % 4, (self.y + k * self.c) % 4
        return (x * 4 + y, self.m)

    def along_b(self, k):
        x, y = (self.x + k * self.c) % 4, (self.y + k * (1 - self.c)) % 4
        return (x * 4 + y, self.m)

    def along_z(self, k):
        return (self.g, ((self.z + k) % 4) * 2 + self.c)

    def along_m(self, k):
        return (self.g, (self.m + k) % 8)

    def sibling(self):
        return (self.g, self.z * 2 + 1 - self.c)

    def block(self, q, j):
        c = self.c
        return 4 * (q * (1 - c) + j * c) + q * c + j * (1 - c)


def remote(src, dst, send, recv, device):
    return pltpu.make_async_remote_copy(
        src_ref=src, dst_ref=dst, send_sem=send, recv_sem=recv, device_id=device, device_id_type=MESH
    )


def greet(devices):
    barrier = pltpu.get_barrier_semaphore()
    for device in devices:
        pl.semaphore_signal(barrier, inc=1, device_id=device, device_id_type=MESH)
    pl.semaphore_wait(barrier, len(devices))


def nt_dot(left, right):
    return lax.dot_general(left, right, (((1,), (1,)), ((), ())), preferred_element_type=F32)


def tn_dot(left, right):
    return lax.dot_general(left, right, (((0,), (0,)), ((), ())), preferred_element_type=F32)


def second(
    scale,
    normed, cot, heads, dproj, w_qkv, w_out, packed, cot_part, mean, rstd, gain,
    output, input_grad, qkv_grad, out_grad,
    cot_a, normed_a, heads_a, dproj_a, wq, wo,
    sib_out, sib_in, z_out, z_in, dn_sib_out, dn_sib_in, dn_z_out, dn_z_in,
    og_out, og_in, qg_out, qg_in, st_out, st_in, st_pad, own_og, own_qg, own_at, own_dn,
    wsem, lsem, cs, cr, ns, nr, hs, hr, ps, pr, ss, sr, zs, zr, dss, dsr, dzs, dzr, os_, or_, qs, qr, ts, tr,
):
    at = Place()
    a, b, c, z, m = at.a, at.b, at.c, at.z, at.m
    width = 768
    half = 384
    load_wo = pltpu.make_async_copy(w_out, wo, wsem.at[0])
    load_wq = pltpu.make_async_copy(w_qkv, wq, wsem.at[1])
    load_wo.start()
    load_wq.start()
    greet([at.along_a(k) for k in (1, 2, 3)] + [at.along_b(k) for k in (1, 2, 3)] + [at.along_m(k) for k in range(1, 8)])

    mine = pl.ds(pl.multiple_of(a * 256, 256), 256)

    def spread(full, buf, send, recv):
        copies = []
        for k in (1, 2, 3):
            q = (a + k) % 4
            for j in range(4):
                cols = pl.ds(pl.multiple_of(at.block(q, j) * half, half), half)
                copies.append(
                    remote(
                        full.at[:, cols], buf.at[mine, pl.ds(j * half, half)],
                        send.at[k - 1, j], recv.at[k - 1, j], at.along_a(k),
                    )
                )
        return copies

    def keep(full, buf, sem):
        copies = []
        for j in range(4):
            cols = pl.ds(pl.multiple_of(at.block(a, j) * half, half), half)
            copies.append(pltpu.make_async_copy(full.at[:, cols], buf.at[mine, pl.ds(j * half, half)], sem.at[j]))
        return copies

    def gather(part, buf, send, recv):
        return [remote(part, buf.at[mine, :], send.at[k - 1], recv.at[k - 1], at.along_a(k)) for k in (1, 2, 3)]

    heads_copies = gather(heads, heads_a, hs, hr)
    cot_copies = spread(cot, cot_a, cs, cr)
    dproj_copies = gather(dproj, dproj_a, ps, pr)
    normed_copies = spread(normed, normed_a, ns, nr)
    local = keep(cot, cot_a, lsem.at[0]) + keep(normed, normed_a, lsem.at[1])
    for copy in heads_copies + cot_copies + dproj_copies + normed_copies + local:
        copy.start()
    heads_a[mine, :] = heads[...]
    dproj_a[mine, :] = dproj[...]

    def attn_term(shard):
        rows = pl.ds(pl.multiple_of(shard * width, width), width)
        return nt_dot(heads[...], wo[rows, :])

    def dn_term(shard):
        rows = pl.ds(pl.multiple_of(shard * width, width), width)
        total = nt_dot(dproj[:, 0:half], wq[0, rows, :])
        total += nt_dot(dproj[:, half : 2 * half], wq[1, rows, :])
        return total + nt_dot(dproj[:, 2 * half : 3 * half], wq[2, rows, :])

    def to_sibling(term, out, into, send, recv):
        def step(k, carry):
            out[k] = term(((z + 1 + k) % 4) * 2 + 1 - c).astype(BF16)
            remote(out.at[k], into.at[k], send.at[k], recv.at[k], at.sibling()).start()
            return carry

        lax.fori_loop(0, 4, step, 0)

    def along_z(term, sib_o, sib, sib_send, sib_recv, out, into, send, recv, own):
        def step(k, carry):
            value = term(((z + 1 + k) % 4) * 2 + c)
            remote(sib_o.at[k], sib.at[k], sib_send.at[k], sib_recv.at[k], at.sibling()).wait()
            out[k] = (value + sib[k].astype(F32)).astype(BF16)
            remote(out.at[k], into.at[k], send.at[k], recv.at[k], at.along_z(1 + k)).start()
            return carry

        lax.fori_loop(0, 3, step, 0)
        value = term(z * 2 + c)
        remote(sib_o.at[3], sib.at[3], sib_send.at[3], sib_recv.at[3], at.sibling()).wait()
        own[...] = value + sib[3].astype(F32)

    load_wo.wait()
    to_sibling(attn_term, sib_out, sib_in, ss, sr)
    load_wq.wait()
    to_sibling(dn_term, dn_sib_out, dn_sib_in, dss, dsr)
    along_z(attn_term, sib_out, sib_in, ss, sr, z_out, z_in, zs, zr, own_at)
    along_z(dn_term, dn_sib_out, dn_sib_in, dss, dsr, dn_z_out, dn_z_in, dzs, dzr, own_dn)

    for copy in local:
        copy.wait()
    for copy in heads_copies + cot_copies:
        copy.wait()

    def out_term(j):
        return tn_dot(cot_a[:, pl.ds(pl.multiple_of(j * half, half), half)], heads_a[...])

    def out_step(k, carry):
        og_out[k] = out_term((b + 1 + k) % 4).astype(BF16)
        remote(og_out.at[k], og_in.at[k], os_.at[k], or_.at[k], at.along_b(1 + k)).start()
        return carry

    lax.fori_loop(0, 3, out_step, 0)
    own_og[...] = out_term(b)

    for copy in dproj_copies + normed_copies:
        copy.wait()

    def qkv_term(j):
        return tn_dot(normed_a[:, pl.ds(pl.multiple_of(j * half, half), half)], dproj_a[...])

    def qkv_step(k, carry):
        qg_out[k] = qkv_term((b + 1 + k) % 4).astype(BF16)
        remote(qg_out.at[k], qg_in.at[k], qs.at[k], qr.at[k], at.along_b(1 + k)).start()
        return carry

    lax.fori_loop(0, 3, qkv_step, 0)
    own_qg[...] = qkv_term(b)

    total = own_at[...]
    for k in range(3):
        remote(z_out.at[k], z_in.at[k], zs.at[k], zr.at[k], at.along_z(1 + k)).wait()
        total += z_in[k].astype(F32)
    output[...] = (packed[...].astype(F32) + total).astype(BF16)

    total = own_dn[...]
    for k in range(3):
        remote(dn_z_out.at[k], dn_z_in.at[k], dzs.at[k], dzr.at[k], at.along_z(1 + k)).wait()
        total += dn_z_in[k].astype(F32)
    u = total * gain[pl.ds(m, 1), :]
    unit = (packed[...].astype(F32) - mean[...]) * rstd[...]
    sum_u = jnp.sum(u, -1, keepdims=True)
    sum_uu = jnp.sum(u * unit, -1, keepdims=True)
    own_dn[...] = u
    lane = lax.broadcasted_iota(jnp.int32, (256, 128), 1)
    pair = jnp.where(lane == 0, sum_u, jnp.where(lane == 1, sum_uu, 0.0))
    st_out[...] = pair.T[0:8]
    stats = [remote(st_out, st_in.at[k - 1], ts.at[k - 1], tr.at[k - 1], at.along_m(k)) for k in range(1, 8)]
    for copy in stats:
        copy.start()
    sums = st_out[...]
    for k in range(7):
        stats[k].wait()
        sums += st_in[k]
    st_pad[...] = jnp.zeros_like(st_pad)
    st_pad[0:8, :] = sums * (1.0 / 6144.0)
    means = st_pad[...].T
    grad = rstd[...] * (own_dn[...] - means[:, 0:1] - unit * means[:, 1:2])
    input_grad[...] = (cot_part[...].astype(F32) + grad).astype(BF16)

    total = own_og[...]
    for k in range(3):
        remote(og_out.at[k], og_in.at[k], os_.at[k], or_.at[k], at.along_b(1 + k)).wait()
        total += og_in[k].astype(F32)
    out_grad[...] = (total * scale).astype(BF16)

    for k in range(3):
        remote(qg_out.at[k], qg_in.at[k], qs.at[k], qr.at[k], at.along_b(1 + k)).wait()
    for t in range(3):
        cols = slice(t * half, (t + 1) * half)
        total = own_qg[:, cols]
        for k in range(3):
            total += qg_in[k, :, cols].astype(F32)
        qkv_grad[t] = (total * scale).astype(BF16)


def call_second(normed, cot, heads, dproj, w_qkv, w_out, packed, cot_part, mean, rstd, gain, scale):
    vmem = pl.BlockSpec(memory_space=pltpu.VMEM)
    anywhere = pl.BlockSpec(memory_space=pl.ANY)
    dma = pltpu.SemaphoreType.DMA
    V = pltpu.VMEM
    return pl.pallas_call(
        functools.partial(second, scale),
        out_shape=(
            jax.ShapeDtypeStruct((256, 768), BF16),
            jax.ShapeDtypeStruct((256, 768), BF16),
            jax.ShapeDtypeStruct((3, 384, 384), BF16),
            jax.ShapeDtypeStruct((384, 384), BF16),
        ),
        in_specs=[anywhere, anywhere, vmem, vmem, anywhere, anywhere, vmem, vmem, vmem, vmem, vmem],
        out_specs=(vmem,) * 4,
        scratch_shapes=[
            V((1024, 1536), BF16), V((1024, 1536), BF16), V((1024, 384), BF16), V((1024, 1152), BF16),
            V((3, 6144, 384), BF16), V((6144, 384), BF16),
            V((4, 256, 768), BF16), V((4, 256, 768), BF16), V((3, 256, 768), BF16), V((3, 256, 768), BF16),
            V((4, 256, 768), BF16), V((4, 256, 768), BF16), V((3, 256, 768), BF16), V((3, 256, 768), BF16),
            V((3, 384, 384), BF16), V((3, 384, 384), BF16), V((3, 384, 1152), BF16), V((3, 384, 1152), BF16),
            V((8, 256), F32), V((7, 8, 256), F32), V((128, 256), F32),
            V((384, 384), F32), V((384, 1152), F32), V((256, 768), F32), V((256, 768), F32),
            dma((2,)), dma((2, 4)), dma((3, 4)), dma((3, 4)), dma((3, 4)), dma((3, 4)),
            dma((3,)), dma((3,)), dma((3,)), dma((3,)),
            dma((4,)), dma((4,)), dma((3,)), dma((3,)), dma((4,)), dma((4,)), dma((3,)), dma((3,)),
            dma((3,)), dma((3,)), dma((3,)), dma((3,)), dma((7,)), dma((7,)),
        ],
        compiler_params=pltpu.CompilerParams(
            collective_id=1, has_side_effects=True, vmem_limit_bytes=62 << 20
        ),
        name="second",
    )(normed, cot, heads, dproj, w_qkv, w_out, packed, cot_part, mean, rstd, gain)


def norm_heads(values, gain):
    center = values - jnp.mean(values, -1, keepdims=True)
    variance = jnp.mean(center * center, -1, keepdims=True)
    return center * lax.rsqrt(variance + 1e-06) * gain


def attend(projected, image_ids, qk_gain):
    row_count = projected.shape[0]
    head_count = projected.shape[2] // DH
    split_heads = projected.reshape(row_count, 3, head_count, DH)
    queries = norm_heads(split_heads[:, 0], qk_gain[0]).astype(jnp.bfloat16)
    keys_normed = norm_heads(split_heads[:, 1], qk_gain[1]).astype(jnp.bfloat16)
    values_bf = split_heads[:, 2].astype(jnp.bfloat16)
    scores = jnp.einsum(
        "qhd,khd->hqk", queries, keys_normed, preferred_element_type=jnp.float32
    ) * DH ** (-0.5)
    same_image = image_ids[:, None] == image_ids[None, :]
    raised = jnp.where(same_image[None], jnp.exp(scores), 0.0)
    weights = (raised / jnp.sum(raised, -1, keepdims=True)).astype(jnp.bfloat16)
    mixed = jnp.einsum("hqk,khd->qhd", weights, values_bf, preferred_element_type=jnp.float32)
    return mixed.reshape(row_count, head_count * DH).astype(jnp.bfloat16)


def contract_rows(left, right):
    return lax.dot_general(
        left, right, (((0,), (0,)), ((), ())), preferred_element_type=jnp.float32
    )


def contract_cols(left, right):
    return lax.dot_general(
        left, right, (((1,), (1,)), ((), ())), preferred_element_type=jnp.float32
    )


def shards(patches, dest_group, dest_row, segment, ln_gain, w_qkv, qk_gain, w_out, cotangent):
    group_rows, part_width = patches.shape
    groups = lax.axis_size("dp")
    slot_size = 2 * group_rows // groups
    full_width, local_width = w_out.shape
    member = (dest_group[:, None] == jnp.arange(groups, dtype=jnp.int32)[None, :]).astype(jnp.int32)
    rank_within = jnp.sum((jnp.cumsum(member, 0) - 1) * member, 1)
    place = dest_group * slot_size + rank_within
    outbox = jnp.zeros((groups * slot_size, part_width), patches.dtype).at[place].set(patches)
    address = jnp.full((groups * slot_size,), group_rows, jnp.int32).at[place].set(dest_row)
    inbox, arrived_at = (
        lax.all_to_all(
            outbox.reshape(groups, slot_size, part_width),
            "dp",
            split_axis=0,
            concat_axis=0,
            tiled=True,
        ),
        lax.all_to_all(
            address.reshape(groups, slot_size), "dp", split_axis=0, concat_axis=0, tiled=True
        ),
    )
    packed = (
        jnp.zeros((group_rows, part_width), patches.dtype)
        .at[arrived_at.reshape(-1)]
        .set(inbox.reshape(-1, part_width), mode="drop")
    )
    whole_rows, whole_cot = (
        lax.all_gather(packed, "mp", axis=1, tiled=True),
        lax.all_gather(cotangent, "mp", axis=1, tiled=True),
    )
    wide = whole_rows.astype(jnp.float32)
    mean = jnp.mean(wide, -1, keepdims=True)
    center = wide - mean
    rstd = lax.rsqrt(jnp.mean(center * center, -1, keepdims=True) + 1e-06)
    unit_rows = center * rstd
    normed = (unit_rows * ln_gain).astype(jnp.bfloat16)
    w_flat = w_qkv.reshape(full_width, 3 * local_width)
    projected = jnp.dot(normed, w_flat, preferred_element_type=jnp.float32).reshape(
        group_rows, 3, local_width
    )
    heads_out, backward = jax.vjp(lambda values: attend(values, segment, qk_gain), projected)
    d_heads = jnp.dot(whole_cot, w_out, preferred_element_type=jnp.float32).astype(jnp.bfloat16)
    (d_projected,) = backward(d_heads)
    d_proj_bf = d_projected.astype(jnp.bfloat16).reshape(group_rows, 3 * local_width)
    scale_grad = 1.0 / math.sqrt(group_rows * groups)
    output, input_grad, qkv_grad, out_grad = call_second(
        normed, whole_cot, heads_out, d_proj_bf, jnp.transpose(w_qkv, (1, 0, 2)), w_out,
        packed, cotangent, mean, rstd, ln_gain.reshape(8, 768), scale_grad,
    )
    return (output, input_grad, jnp.transpose(qkv_grad, (1, 0, 2)), out_grad)


def solution(mesh):
    placed = (
        P("dp", "mp"),
        P("dp"),
        P("dp"),
        P("dp"),
        P(),
        P(None, None, "mp"),
        P(),
        P(None, "mp"),
        P("dp", "mp"),
    )
    return jax.shard_map(
        shards,
        mesh=mesh,
        in_specs=placed,
        out_specs=(P("dp", "mp"), P("dp", "mp"), P("dp", None, "mp"), P("dp", "mp")),
        check_vma=False,
    )
```

```python
import functools
import math

import jax
import jax.numpy as jnp
from jax import lax
from jax.experimental import pallas as pl
from jax.experimental.pallas import tpu as pltpu
from jax.sharding import PartitionSpec as P

DH = 128
MESH = pl.DeviceIdType.MESH
F32 = jnp.float32
BF16 = jnp.bfloat16


class Place:
    def __init__(self):
        self.g, self.m = lax.axis_index("dp"), lax.axis_index("mp")
        self.x, self.y = self.g // 4, self.g % 4
        self.z, self.c = self.m // 2, self.m % 2
        c = self.c
        self.a = self.x * (1 - c) + self.y * c
        self.b = self.x * c + self.y * (1 - c)

    def along_a(self, k):
        x, y = (self.x + k * (1 - self.c)) % 4, (self.y + k * self.c) % 4
        return (x * 4 + y, self.m)

    def along_b(self, k):
        x, y = (self.x + k * self.c) % 4, (self.y + k * (1 - self.c)) % 4
        return (x * 4 + y, self.m)

    def along_z(self, k):
        return (self.g, ((self.z + k) % 4) * 2 + self.c)

    def along_m(self, k):
        return (self.g, (self.m + k) % 8)

    def over_xy(self, dx, dy):
        return (((self.x + dx) % 4) * 4 + (self.y + dy) % 4, self.m)

    def sibling(self):
        return (self.g, self.z * 2 + 1 - self.c)

    def block(self, q, j):
        c = self.c
        return 4 * (q * (1 - c) + j * c) + q * c + j * (1 - c)


def remote(src, dst, send, recv, device):
    return pltpu.make_async_remote_copy(
        src_ref=src, dst_ref=dst, send_sem=send, recv_sem=recv, device_id=device, device_id_type=MESH
    )


def nt_dot(left, right):
    return lax.dot_general(left, right, (((1,), (1,)), ((), ())), preferred_element_type=F32)


def tn_dot(left, right):
    return lax.dot_general(left, right, (((0,), (0,)), ((), ())), preferred_element_type=F32)


def whole(
    scale,
    patches, dest_group, dest_row, segment, gain, w_qkv, qk_gain, w_out, cot,
    output, input_grad, qkv_grad, out_grad,
    outbox, inbox, packed, cot_full, normed_full, cot_a, normed_a, heads_a, dproj_a, wq, wo,
    proj, d_heads, heads, dproj, columns, places, st_pad, st_out, st_in, en_out, en_in,
    sib_in, z_in, dn_sib_out, dn_sib_in, dn_z_out, dn_z_in, og_in, qg_in,
    own_og, own_qg, own_at, own_dn,
    wsem, rs, rr, cz, czr, cb, cbr, nz, nzr, nb, nbr, sts, str_, ens, enr,
    cs, cr, cl, ns, nr, nl, hs, hr, ps, pr, ss, sr, zs, zr, dss, dsr, dzs, dzr, os_, or_, qs, qr,
):
    at = Place()
    a, b, c, z, m, g = at.a, at.b, at.c, at.z, at.m, at.g
    width, half, rows = 768, 384, 256
    load_wo = pltpu.make_async_copy(w_out, wo, wsem.at[0])
    load_wq = pltpu.make_async_copy(w_qkv, wq, wsem.at[1])
    load_wo.start()
    load_wq.start()
    over_dp = [(dx, dy) for dx in range(4) for dy in range(4) if dx + dy > 0]
    barrier = pltpu.get_barrier_semaphore()
    met = [at.over_xy(dx, dy) for dx, dy in over_dp] + [at.along_m(k) for k in range(1, 8)]
    for device in met:
        pl.semaphore_signal(barrier, inc=1, device_id=device, device_id_type=MESH)

    group_row = dest_group[...]
    member = (lax.broadcasted_iota(jnp.int32, (16, rows), 0) == group_row).astype(F32)
    before = (
        lax.broadcasted_iota(jnp.int32, (rows, rows), 0) < lax.broadcasted_iota(jnp.int32, (rows, rows), 1)
    ).astype(BF16)
    rank = jnp.sum(jnp.dot(member.astype(BF16), before, preferred_element_type=F32) * member, 0, keepdims=True)
    slot = group_row.astype(F32) * 32.0 + rank
    pick = (lax.broadcasted_iota(jnp.int32, (512, rows), 0).astype(F32) == slot).astype(BF16)
    st_pad[...] = jnp.zeros_like(st_pad)
    st_pad[0:1, :] = dest_row[...].astype(F32) + 1.0
    st_pad[1:2, :] = segment[...].astype(F32)
    places[...] = st_pad[...].T
    address = jnp.broadcast_to(places[:, 0:1], (rows, 128)).astype(BF16)
    outbox[:, 0:width] = jnp.dot(pick, patches[...], preferred_element_type=F32).astype(BF16)
    outbox[:, width:] = jnp.dot(pick, address, preferred_element_type=F32).astype(BF16)
    cot_full[m] = cot[...]
    pl.semaphore_wait(barrier, len(met))

    here = pl.ds(pl.multiple_of(g * 32, 32), 32)
    routes = []
    for i, (dx, dy) in enumerate(over_dp):
        device = at.over_xy(dx, dy)
        there = pl.ds(pl.multiple_of(device[0] * 32, 32), 32)
        routes.append(remote(outbox.at[there, :], inbox.at[here, :], rs.at[i], rr.at[i], device))
    for copy in routes:
        copy.start()
    inbox[here, :] = outbox[here, :]

    class Collect:
        def __init__(self, full, z_send, z_recv, b_send, b_recv):
            self.full, self.b_send, self.b_recv = full, b_send, b_recv
            self.z = [
                remote(full.at[m], full.at[m], z_send.at[k - 1], z_recv.at[k - 1], at.along_z(k)) for k in (1, 2, 3)
            ]
            self.b = [self.across(k) for k in range(4)]

        def across(self, k):
            s = self.mine(k)
            return remote(self.full.at[s], self.full.at[s], self.b_send.at[k], self.b_recv.at[k], at.sibling())

        def mine(self, k):
            return ((z + 4 - k) % 4) * 2 + c

        def others(self, k):
            return ((z + 4 - k) % 4) * 2 + 1 - c

        def start(self):
            for k in (1, 3, 2):
                self.z[k - 1].start()
            self.b[0].start()

        def arrive(self, k):
            if k > 0:
                self.z[k - 1].wait_recv()
                self.b[k].start()

        def arrive_other(self, k):
            self.b[k].wait_recv()

        def finish(self):
            for copy in self.z + self.b:
                copy.wait_send()

    mine = pl.ds(pl.multiple_of(a * rows, rows), rows)

    def spread_slab(full, s, buf, send, recv, near):
        for h in (0, 1):
            bx, by = (2 * s + h) // 4, (2 * s + h) % 4
            q, j = bx * (1 - c) + by * c, bx * c + by * (1 - c)
            k = (q - a + 4) % 4
            n = (k + 3) % 4
            src = full.at[s, :, pl.ds(h * half, half)]
            dst = buf.at[mine, pl.ds(pl.multiple_of(j * half, half), half)]

            @pl.when(k == 0)
            def _():
                pltpu.make_async_copy(src, dst, near.at[j]).start()

            @pl.when(k != 0)
            def _():
                remote(src, dst, send.at[n, j], recv.at[n, j], at.along_a(k)).start()

    def spread_ends(full, buf, send, recv, near):
        far = [
            remote(full.at[0, :, 0:half], buf.at[mine, 0:half], send.at[k - 1, j], recv.at[k - 1, j], at.along_a(k))
            for k in (1, 2, 3)
            for j in range(4)
        ]
        local = [pltpu.make_async_copy(full.at[0, :, 0:half], buf.at[mine, 0:half], near.at[j]) for j in range(4)]
        return far, local

    def shard_rows(s):
        return pl.ds(pl.multiple_of(s * width, width), width)

    cots = Collect(cot_full, cz, czr, cb, cbr)
    cots.start()
    load_wo.wait()

    def add_heads(s, first=False):
        term = jnp.dot(cot_full[s], wo[shard_rows(s), :], preferred_element_type=F32)
        d_heads[...] = term if first else d_heads[...] + term

    add_heads(m, True)
    cots.arrive_other(0)
    add_heads(cots.others(0))
    for k in (1, 3):
        cots.arrive(k)
        add_heads(cots.mine(k))
        cots.arrive_other(k)
        add_heads(cots.others(k))

    for copy in routes:
        copy.wait()
    arrived = inbox[:, width : width + 1].astype(F32)
    put = (lax.broadcasted_iota(jnp.int32, (512, rows), 1).astype(F32) + 1.0 == arrived).astype(BF16)
    block = tn_dot(put, inbox[:, 0:width])
    packed[...] = block.astype(BF16)

    def exchange(first, second, out, into, send, recv):
        lane = lax.broadcasted_iota(jnp.int32, (rows, 128), 1)
        out[...] = jnp.where(lane == 0, first, jnp.where(lane == 1, second, 0.0)).T[0:8]
        return [remote(out, into.at[k - 1], send.at[k - 1], recv.at[k - 1], at.along_m(k)) for k in range(1, 8)]

    part_mean = jnp.mean(block, -1, keepdims=True)
    part_center = block - part_mean
    stats = exchange(part_mean, jnp.sum(part_center * part_center, -1, keepdims=True), st_out, st_in, sts, str_)
    for copy in stats:
        copy.start()

    for k in (0, 1, 3):
        spread_slab(cot_full, cots.mine(k), cot_a, cs, cr, cl)
        spread_slab(cot_full, cots.others(k), cot_a, cs, cr, cl)
    for copy in stats:
        copy.wait()
    parts = [st_out[...]] + [st_in[k] for k in range(7)]
    mean = sum(part[0:1] for part in parts) * 0.125
    spread = sum(part[1:2] + width * (part[0:1] - mean) * (part[0:1] - mean) for part in parts)
    st_pad[0:1, :] = mean
    st_pad[1:2, :] = lax.rsqrt(spread * (1.0 / 6144.0) + 1e-06)
    columns[...] = st_pad[...].T
    gain_part = gain[:, pl.ds(pl.multiple_of(m * width, width), width)]
    unit = (packed[...].astype(F32) - columns[:, 0:1]) * columns[:, 1:2]
    normed_full[m] = (unit * gain_part).astype(BF16)
    norms = Collect(normed_full, nz, nzr, nb, nbr)
    norms.start()

    cots.arrive(2)
    spread_slab(cot_full, cots.mine(2), cot_a, cs, cr, cl)
    add_heads(cots.mine(2))
    cots.arrive_other(2)
    spread_slab(cot_full, cots.others(2), cot_a, cs, cr, cl)
    add_heads(cots.others(2))
    load_wq.wait()

    def add_projected(s, first=False):
        spread_slab(normed_full, s, normed_a, ns, nr, nl)
        for t in range(3):
            cols = slice(t * half, (t + 1) * half)
            term = jnp.dot(normed_full[s], wq[t, shard_rows(s), :], preferred_element_type=F32)
            proj[:, cols] = term if first else proj[:, cols] + term

    add_projected(m, True)
    norms.arrive_other(0)
    add_projected(norms.others(0))
    for k in (1, 3, 2):
        norms.arrive(k)
        add_projected(norms.mine(k))
        norms.arrive_other(k)
        add_projected(norms.others(k))

    same = places[:, 1:2] == segment[...].astype(F32)

    def normalise(values):
        center = values - jnp.mean(values, -1, keepdims=True)
        inverse = lax.rsqrt(jnp.mean(center * center, -1, keepdims=True) + 1e-06)
        return center * inverse, inverse

    def normalise_back(grad, unit, inverse, weight):
        scaled = grad.astype(BF16).astype(F32) * weight
        inner = scaled - jnp.mean(scaled, -1, keepdims=True) - unit * jnp.mean(scaled * unit, -1, keepdims=True)
        return (inverse * inner).astype(BF16)

    root = DH ** (-0.5)
    for h in range(3):
        q_cols, k_cols, v_cols = (slice(t * half + h * DH, t * half + (h + 1) * DH) for t in range(3))
        h_cols = slice(h * DH, (h + 1) * DH)
        unit_q, inverse_q = normalise(proj[:, q_cols])
        unit_k, inverse_k = normalise(proj[:, k_cols])
        queries = (unit_q * qk_gain[0:1, :]).astype(BF16)
        keys = (unit_k * qk_gain[1:2, :]).astype(BF16)
        values = proj[:, v_cols].astype(BF16)
        raised = jnp.where(same, jnp.exp(nt_dot(queries, keys) * root), 0.0)
        exact = raised / jnp.sum(raised, -1, keepdims=True)
        weights = exact.astype(BF16)
        heads[:, h_cols] = jnp.dot(weights, values, preferred_element_type=F32).astype(BF16)
        given = d_heads[:, h_cols].astype(BF16)
        d_weights = nt_dot(given, values).astype(BF16).astype(F32)
        dproj[:, v_cols] = tn_dot(weights, given).astype(BF16)
        inner = jnp.sum(d_weights * exact, -1, keepdims=True)
        d_scores = (exact * (d_weights - inner) * root).astype(BF16)
        d_queries = jnp.dot(d_scores, keys, preferred_element_type=F32)
        d_keys = tn_dot(d_scores, queries)
        dproj[:, q_cols] = normalise_back(d_queries, unit_q, inverse_q, qk_gain[0:1, :])
        dproj[:, k_cols] = normalise_back(d_keys, unit_k, inverse_k, qk_gain[1:2, :])

    def gather(part, buf, send, recv):
        return [remote(part, buf.at[mine, :], send.at[k - 1], recv.at[k - 1], at.along_a(k)) for k in (1, 2, 3)]

    heads_copies = gather(heads, heads_a, hs, hr)
    dproj_copies = gather(dproj, dproj_a, ps, pr)
    for copy in heads_copies + dproj_copies:
        copy.start()
    heads_a[mine, :] = heads[...]
    dproj_a[mine, :] = dproj[...]
    cots.finish()
    cot_far, cot_near = spread_ends(cot_full, cot_a, cs, cr, cl)
    for copy in cot_far:
        copy.wait_send()
    for copy in cot_near:
        copy.wait()

    sib_out, z_out = cot_full.at[0:4], cot_full.at[4:7]
    def attn_term(shard):
        rows = shard_rows(shard)
        return nt_dot(heads[...], wo[rows, :])

    def dn_term(shard):
        rows = shard_rows(shard)
        total = nt_dot(dproj[:, 0:half], wq[0, rows, :])
        total += nt_dot(dproj[:, half : 2 * half], wq[1, rows, :])
        return total + nt_dot(dproj[:, 2 * half : 3 * half], wq[2, rows, :])

    def to_sibling(term, out, into, send, recv):
        def step(k, carry):
            out[k] = term(((z + 1 + k) % 4) * 2 + 1 - c).astype(BF16)
            remote(out.at[k], into.at[k], send.at[k], recv.at[k], at.sibling()).start()
            return carry

        lax.fori_loop(0, 4, step, 0)

    def along_z(term, sib_o, sib, sib_send, sib_recv, out, into, send, recv, own):
        def step(k, carry):
            value = term(((z + 1 + k) % 4) * 2 + c)
            remote(sib_o.at[k], sib.at[k], sib_send.at[k], sib_recv.at[k], at.sibling()).wait()
            out[k] = (value + sib[k].astype(F32)).astype(BF16)
            remote(out.at[k], into.at[k], send.at[k], recv.at[k], at.along_z(1 + k)).start()
            return carry

        lax.fori_loop(0, 3, step, 0)
        value = term(z * 2 + c)
        remote(sib_o.at[3], sib.at[3], sib_send.at[3], sib_recv.at[3], at.sibling()).wait()
        own[...] = value + sib[3].astype(F32)

    to_sibling(attn_term, sib_out, sib_in, ss, sr)
    to_sibling(dn_term, dn_sib_out, dn_sib_in, dss, dsr)
    along_z(attn_term, sib_out, sib_in, ss, sr, z_out, z_in, zs, zr, own_at)
    along_z(dn_term, dn_sib_out, dn_sib_in, dss, dsr, dn_z_out, dn_z_in, dzs, dzr, own_dn)

    for copy in heads_copies:
        copy.wait()
    for copy in cot_far:
        copy.wait_recv()

    og_out = [wo.at[pl.ds(3456 + half * k, half), :] for k in range(3)]
    qg_out = [wo.at[pl.ds(1152 * k, 1152), :] for k in range(3)]

    def out_term(j):
        return tn_dot(cot_a[:, pl.ds(pl.multiple_of(j * half, half), half)], heads_a[...])

    og_copies = [remote(og_out[k], og_in.at[k], os_.at[k], or_.at[k], at.along_b(1 + k)) for k in range(3)]
    qg_copies = [remote(qg_out[k], qg_in.at[k], qs.at[k], qr.at[k], at.along_b(1 + k)) for k in range(3)]

    def out_step(k, carry):
        to = pl.ds(pl.multiple_of(3456 + half * k, half), half)
        wo[to, :] = out_term((b + 1 + k) % 4).astype(BF16)
        remote(wo.at[to, :], og_in.at[k], os_.at[k], or_.at[k], at.along_b(1 + k)).start()
        return carry

    lax.fori_loop(0, 3, out_step, 0)
    own_og[...] = out_term(b)

    norms.finish()
    normed_far, normed_near = spread_ends(normed_full, normed_a, ns, nr, nl)
    for copy in dproj_copies + normed_far + normed_near:
        copy.wait()

    def qkv_term(j):
        return tn_dot(normed_a[:, pl.ds(pl.multiple_of(j * half, half), half)], dproj_a[...])

    def qkv_step(k, carry):
        term = qkv_term((b + 1 + k) % 4).astype(BF16)
        for t in range(3):
            wo[pl.ds(pl.multiple_of(1152 * k + half * t, half), half), :] = term[:, t * half : (t + 1) * half]
        to = pl.ds(pl.multiple_of(1152 * k, half), 1152)
        remote(wo.at[to, :], qg_in.at[k], qs.at[k], qr.at[k], at.along_b(1 + k)).start()
        return carry

    lax.fori_loop(0, 3, qkv_step, 0)
    own_qg[...] = qkv_term(b)

    total = own_at[...]
    for k in range(3):
        remote(z_out.at[k], z_in.at[k], zs.at[k], zr.at[k], at.along_z(1 + k)).wait()
        total += z_in[k].astype(F32)
    output[...] = (packed[...].astype(F32) + total).astype(BF16)

    total = own_dn[...]
    for k in range(3):
        remote(dn_z_out.at[k], dn_z_in.at[k], dzs.at[k], dzr.at[k], at.along_z(1 + k)).wait()
        total += dn_z_in[k].astype(F32)
    rstd = columns[:, 1:2]
    unit = (packed[...].astype(F32) - columns[:, 0:1]) * rstd
    u = total * gain_part
    own_dn[...] = u
    ends = exchange(jnp.sum(u, -1, keepdims=True), jnp.sum(u * unit, -1, keepdims=True), en_out, en_in, ens, enr)
    for copy in ends:
        copy.start()
    for copy in ends:
        copy.wait()
    st_pad[0:8, :] = (en_out[...] + sum(en_in[k] for k in range(7))) * (1.0 / 6144.0)
    means = st_pad[...].T
    unit = (packed[...].astype(F32) - columns[:, 0:1]) * rstd
    grad = rstd * (own_dn[...] - means[:, 0:1] - unit * means[:, 1:2])
    input_grad[...] = (cot[...].astype(F32) + grad).astype(BF16)

    for copy in og_copies:
        copy.wait()
    out_grad[...] = ((own_og[...] + sum(og_in[k].astype(F32) for k in range(3))) * scale).astype(BF16)
    for copy in qg_copies:
        copy.wait()
    for t in range(3):
        part = slice(t * half, (t + 1) * half)
        total = own_qg[:, part] + sum(qg_in[k, part, :].astype(F32) for k in range(3))
        qkv_grad[t] = (total * scale).astype(BF16)


def shards(patches, dest_group, dest_row, segment, ln_gain, w_qkv, qk_gain, w_out, cotangent):
    vmem = pl.BlockSpec(memory_space=pltpu.VMEM)
    anywhere = pl.BlockSpec(memory_space=pl.ANY)
    dma = pltpu.SemaphoreType.DMA
    V = pltpu.VMEM
    scale = 1.0 / math.sqrt(4096)
    output, input_grad, qkv_grad, out_grad = pl.pallas_call(
        functools.partial(whole, scale),
        out_shape=(
            jax.ShapeDtypeStruct((256, 768), BF16),
            jax.ShapeDtypeStruct((256, 768), BF16),
            jax.ShapeDtypeStruct((3, 384, 384), BF16),
            jax.ShapeDtypeStruct((384, 384), BF16),
        ),
        in_specs=[vmem, vmem, vmem, vmem, vmem, anywhere, vmem, anywhere, vmem],
        out_specs=(vmem,) * 4,
        scratch_shapes=[
            V((512, 896), BF16), V((512, 896), BF16), V((256, 768), BF16),
            V((8, 256, 768), BF16), V((8, 256, 768), BF16),
            V((1024, 1536), BF16), V((1024, 1536), BF16), V((1024, 384), BF16), V((1024, 1152), BF16),
            V((3, 6144, 384), BF16), V((6144, 384), BF16),
            V((256, 1152), F32), V((256, 384), F32), V((256, 384), BF16), V((256, 1152), BF16),
            V((256, 128), F32), V((256, 128), F32), V((128, 256), F32),
            V((8, 256), F32), V((7, 8, 256), F32), V((8, 256), F32), V((7, 8, 256), F32),
            V((4, 256, 768), BF16), V((3, 256, 768), BF16),
            V((4, 256, 768), BF16), V((4, 256, 768), BF16), V((3, 256, 768), BF16), V((3, 256, 768), BF16),
            V((3, 384, 384), BF16), V((3, 1152, 384), BF16),
            V((384, 384), F32), V((384, 1152), F32), V((256, 768), F32), V((256, 768), F32),
            dma((2,)), dma((15,)), dma((15,)),
            dma((3,)), dma((3,)), dma((4,)), dma((4,)), dma((3,)), dma((3,)), dma((4,)), dma((4,)),
            dma((7,)), dma((7,)), dma((7,)), dma((7,)),
            dma((3, 4)), dma((3, 4)), dma((4,)), dma((3, 4)), dma((3, 4)), dma((4,)),
            dma((3,)), dma((3,)), dma((3,)), dma((3,)),
            dma((4,)), dma((4,)), dma((3,)), dma((3,)), dma((4,)), dma((4,)), dma((3,)), dma((3,)),
            dma((3,)), dma((3,)), dma((3,)), dma((3,)),
        ],
        compiler_params=pltpu.CompilerParams(
            collective_id=1, has_side_effects=True, vmem_limit_bytes=62 << 20
        ),
        name="whole",
    )(
        patches, dest_group.reshape(1, 256), dest_row.reshape(1, 256), segment.reshape(1, 256),
        ln_gain.reshape(1, 6144), jnp.transpose(w_qkv, (1, 0, 2)), qk_gain, w_out, cotangent,
    )
    return (output, input_grad, jnp.transpose(qkv_grad, (1, 0, 2)), out_grad)


def solution(mesh):
    placed = (
        P("dp", "mp"),
        P("dp"),
        P("dp"),
        P("dp"),
        P(),
        P(None, None, "mp"),
        P(),
        P(None, "mp"),
        P("dp", "mp"),
    )
    return jax.shard_map(
        shards,
        mesh=mesh,
        in_specs=placed,
        out_specs=(P("dp", "mp"), P("dp", "mp"), P("dp", None, "mp"), P("dp", "mp")),
        check_vma=False,
    )
```

```python
import functools
import math

import jax
import jax.numpy as jnp
from jax import lax
from jax.experimental import pallas as pl
from jax.experimental.pallas import tpu as pltpu
from jax.sharding import PartitionSpec as P

DH = 128
MESH = pl.DeviceIdType.MESH
F32 = jnp.float32
BF16 = jnp.bfloat16


class Place:
    def __init__(self):
        self.g, self.m = lax.axis_index("dp"), lax.axis_index("mp")
        self.x, self.y = self.g // 4, self.g % 4
        self.z, self.c = self.m // 2, self.m % 2
        c = self.c
        self.a = self.x * (1 - c) + self.y * c
        self.b = self.x * c + self.y * (1 - c)

    def along_a(self, k):
        x, y = (self.x + k * (1 - self.c)) % 4, (self.y + k * self.c) % 4
        return (x * 4 + y, self.m)

    def along_b(self, k):
        x, y = (self.x + k * self.c) % 4, (self.y + k * (1 - self.c)) % 4
        return (x * 4 + y, self.m)

    def along_z(self, k):
        return (self.g, ((self.z + k) % 4) * 2 + self.c)

    def along_m(self, k):
        return (self.g, (self.m + k) % 8)

    def over_xy(self, dx, dy):
        return (((self.x + dx) % 4) * 4 + (self.y + dy) % 4, self.m)

    def sibling(self):
        return (self.g, self.z * 2 + 1 - self.c)

    def block(self, q, j):
        c = self.c
        return 4 * (q * (1 - c) + j * c) + q * c + j * (1 - c)


def remote(src, dst, send, recv, device):
    return pltpu.make_async_remote_copy(
        src_ref=src, dst_ref=dst, send_sem=send, recv_sem=recv, device_id=device, device_id_type=MESH
    )


def nt_dot(left, right):
    return lax.dot_general(left, right, (((1,), (1,)), ((), ())), preferred_element_type=F32)


def tn_dot(left, right):
    return lax.dot_general(left, right, (((0,), (0,)), ((), ())), preferred_element_type=F32)


def whole(
    scale,
    patches, dest_group, dest_row, segment, gain, w_qkv, qk_gain, w_out, cot,
    output, input_grad, qkv_grad, out_grad,
    outbox, inbox, packed, cot_full, normed_full, cot_a, normed_a, parts_a, wq, wo,
    proj, d_heads, heads, dproj, columns, places, st_pad, st_out, st_in, en_out, en_in,
    sib_in, z_in, dn_sib_out, dn_sib_in, dn_z_out, dn_z_in, far_in, near_in,
    own_part, own_at, own_dn,
    wsem, rs, rr, cz, czr, cb, cbr, nz, nzr, nb, nbr, sts, str_, ens, enr,
    cs, cr, cl, ns, nr, nl, gs, gr, ss, sr, zs, zr, dss, dsr, dzs, dzr, qs, qr,
):
    at = Place()
    a, b, c, z, m, g = at.a, at.b, at.c, at.z, at.m, at.g
    width, half, rows = 768, 384, 256
    load_wo = pltpu.make_async_copy(w_out, wo, wsem.at[0])
    load_wq = pltpu.make_async_copy(w_qkv, wq, wsem.at[1])
    load_wo.start()
    load_wq.start()
    over_dp = [(dx, dy) for dx in range(4) for dy in range(4) if dx + dy > 0]
    barrier = pltpu.get_barrier_semaphore()
    met = [at.over_xy(dx, dy) for dx, dy in over_dp] + [at.along_m(k) for k in range(1, 8)]
    for device in met:
        pl.semaphore_signal(barrier, inc=1, device_id=device, device_id_type=MESH)

    group_row = dest_group[...]
    member = (lax.broadcasted_iota(jnp.int32, (16, rows), 0) == group_row).astype(F32)
    before = (
        lax.broadcasted_iota(jnp.int32, (rows, rows), 0) < lax.broadcasted_iota(jnp.int32, (rows, rows), 1)
    ).astype(BF16)
    rank = jnp.sum(jnp.dot(member.astype(BF16), before, preferred_element_type=F32) * member, 0, keepdims=True)
    slot = group_row.astype(F32) * 32.0 + rank
    pick = (lax.broadcasted_iota(jnp.int32, (512, rows), 0).astype(F32) == slot).astype(BF16)
    st_pad[...] = jnp.zeros_like(st_pad)
    st_pad[0:1, :] = dest_row[...].astype(F32) + 1.0
    st_pad[1:2, :] = segment[...].astype(F32)
    places[...] = st_pad[...].T
    address = jnp.broadcast_to(places[:, 0:1], (rows, 128)).astype(BF16)
    outbox[:, 0:width] = jnp.dot(pick, patches[...], preferred_element_type=F32).astype(BF16)
    outbox[:, width:] = jnp.dot(pick, address, preferred_element_type=F32).astype(BF16)
    cot_full[m] = cot[...]
    pl.semaphore_wait(barrier, len(met))

    here = pl.ds(pl.multiple_of(g * 32, 32), 32)
    routes = []
    for i, (dx, dy) in enumerate(over_dp):
        device = at.over_xy(dx, dy)
        there = pl.ds(pl.multiple_of(device[0] * 32, 32), 32)
        routes.append(remote(outbox.at[there, :], inbox.at[here, :], rs.at[i], rr.at[i], device))
    for copy in routes:
        copy.start()
    inbox[here, :] = outbox[here, :]

    class Collect:
        def __init__(self, full, z_send, z_recv, b_send, b_recv):
            up, down = at.along_z(1), at.along_z(3)
            own, low, high = full.at[m], full.at[self.mine(1), 0:128, :], full.at[self.mine(3), 128:256, :]
            self.z = [
                remote(src, src, z_send.at[i], z_recv.at[i], to)
                for i, (src, to) in enumerate([(own, up), (own, down), (low, up), (high, down)])
            ]
            slabs = [full.at[self.mine(k)] for k in range(4)]
            self.b = [remote(slabs[k], slabs[k], b_send.at[k], b_recv.at[k], at.sibling()) for k in range(4)]

        def mine(self, k):
            return ((z + 4 - k) % 4) * 2 + c

        def others(self, k):
            return ((z + 4 - k) % 4) * 2 + 1 - c

        def start(self):
            self.z[0].start()
            self.z[1].start()
            self.b[0].start()

        def arrive(self, k):
            if k == 2:
                self.z[2].wait_recv()
                self.z[3].wait_recv()
            else:
                self.z[k // 2].wait_recv()
                self.z[2 + k // 2].start()
            self.b[k].start()

        def arrive_other(self, k):
            self.b[k].wait_recv()

        def finish(self):
            for copy in self.z + self.b:
                copy.wait_send()

    mine = pl.ds(pl.multiple_of(a * rows, rows), rows)

    def spread_slab(full, s, buf, send, recv, near):
        for h in (0, 1):
            bx, by = (2 * s + h) // 4, (2 * s + h) % 4
            q, j = bx * (1 - c) + by * c, bx * c + by * (1 - c)
            k = (q - a + 4) % 4
            n = (k + 3) % 4
            src = full.at[s, :, pl.ds(h * half, half)]
            dst = buf.at[mine, pl.ds(pl.multiple_of(j * half, half), half)]

            @pl.when(k == 0)
            def _():
                pltpu.make_async_copy(src, dst, near.at[j]).start()

            @pl.when(k != 0)
            def _():
                remote(src, dst, send.at[n, j], recv.at[n, j], at.along_a(k)).start()

    def spread_ends(full, buf, send, recv, near):
        far = [
            remote(full.at[0, :, 0:half], buf.at[mine, 0:half], send.at[k - 1, j], recv.at[k - 1, j], at.along_a(k))
            for k in (1, 2, 3)
            for j in range(4)
        ]
        local = [pltpu.make_async_copy(full.at[0, :, 0:half], buf.at[mine, 0:half], near.at[j]) for j in range(4)]
        return far, local

    def shard_rows(s):
        return pl.ds(pl.multiple_of(s * width, width), width)

    cots = Collect(cot_full, cz, czr, cb, cbr)
    cots.start()
    load_wo.wait()

    def add_heads(s, first=False):
        term = jnp.dot(cot_full[s], wo[shard_rows(s), :], preferred_element_type=F32)
        d_heads[...] = term if first else d_heads[...] + term

    add_heads(m, True)
    cots.arrive_other(0)
    add_heads(cots.others(0))
    cots.arrive(1)
    cots.arrive(3)
    for k in (1, 3):
        add_heads(cots.mine(k))
        cots.arrive_other(k)
        add_heads(cots.others(k))

    for copy in routes:
        copy.wait()
    arrived = inbox[:, width : width + 1].astype(F32)
    put = (lax.broadcasted_iota(jnp.int32, (512, rows), 1).astype(F32) + 1.0 == arrived).astype(BF16)
    block = tn_dot(put, inbox[:, 0:width])
    packed[...] = block.astype(BF16)

    def exchange(first, second, out, into, send, recv):
        lane = lax.broadcasted_iota(jnp.int32, (rows, 128), 1)
        out[...] = jnp.where(lane == 0, first, jnp.where(lane == 1, second, 0.0)).T[0:8]
        return [remote(out, into.at[k - 1], send.at[k - 1], recv.at[k - 1], at.along_m(k)) for k in range(1, 8)]

    part_mean = jnp.mean(block, -1, keepdims=True)
    part_center = block - part_mean
    stats = exchange(part_mean, jnp.sum(part_center * part_center, -1, keepdims=True), st_out, st_in, sts, str_)
    for copy in stats:
        copy.start()

    for k in (0, 1, 3):
        spread_slab(cot_full, cots.mine(k), cot_a, cs, cr, cl)
        spread_slab(cot_full, cots.others(k), cot_a, cs, cr, cl)
    for copy in stats:
        copy.wait()
    parts = [st_out[...]] + [st_in[k] for k in range(7)]
    mean = sum(part[0:1] for part in parts) * 0.125
    spread = sum(part[1:2] + width * (part[0:1] - mean) * (part[0:1] - mean) for part in parts)
    st_pad[0:1, :] = mean
    st_pad[1:2, :] = lax.rsqrt(spread * (1.0 / 6144.0) + 1e-06)
    columns[...] = st_pad[...].T
    gain_part = gain[:, pl.ds(pl.multiple_of(m * width, width), width)]
    unit = (packed[...].astype(F32) - columns[:, 0:1]) * columns[:, 1:2]
    normed_full[m] = (unit * gain_part).astype(BF16)
    norms = Collect(normed_full, nz, nzr, nb, nbr)
    norms.start()

    cots.arrive(2)
    spread_slab(cot_full, cots.mine(2), cot_a, cs, cr, cl)
    add_heads(cots.mine(2))
    cots.arrive_other(2)
    spread_slab(cot_full, cots.others(2), cot_a, cs, cr, cl)
    add_heads(cots.others(2))
    load_wq.wait()

    def add_projected(s, first=False):
        spread_slab(normed_full, s, normed_a, ns, nr, nl)
        for t in range(3):
            cols = slice(t * half, (t + 1) * half)
            term = jnp.dot(normed_full[s], wq[t, shard_rows(s), :], preferred_element_type=F32)
            proj[:, cols] = term if first else proj[:, cols] + term

    add_projected(m, True)
    norms.arrive_other(0)
    add_projected(norms.others(0))
    norms.arrive(1)
    norms.arrive(3)
    for k in (1, 3):
        add_projected(norms.mine(k))
        norms.arrive_other(k)
        add_projected(norms.others(k))
    norms.arrive(2)
    add_projected(norms.mine(2))
    norms.arrive_other(2)
    add_projected(norms.others(2))

    same = places[:, 1:2] == segment[...].astype(F32)

    def normalise(values):
        center = values - jnp.mean(values, -1, keepdims=True)
        inverse = lax.rsqrt(jnp.mean(center * center, -1, keepdims=True) + 1e-06)
        return center * inverse, inverse

    def normalise_back(grad, unit, inverse, weight):
        scaled = grad.astype(BF16).astype(F32) * weight
        inner = scaled - jnp.mean(scaled, -1, keepdims=True) - unit * jnp.mean(scaled * unit, -1, keepdims=True)
        return (inverse * inner).astype(BF16)

    root = DH ** (-0.5)
    for h in range(3):
        q_cols, k_cols, v_cols = (slice(t * half + h * DH, t * half + (h + 1) * DH) for t in range(3))
        h_cols = slice(h * DH, (h + 1) * DH)
        unit_q, inverse_q = normalise(proj[:, q_cols])
        unit_k, inverse_k = normalise(proj[:, k_cols])
        queries = (unit_q * qk_gain[0:1, :]).astype(BF16)
        keys = (unit_k * qk_gain[1:2, :]).astype(BF16)
        values = proj[:, v_cols].astype(BF16)
        raised = jnp.where(same, jnp.exp(nt_dot(queries, keys) * root), 0.0)
        exact = raised / jnp.sum(raised, -1, keepdims=True)
        weights = exact.astype(BF16)
        heads[:, h_cols] = jnp.dot(weights, values, preferred_element_type=F32).astype(BF16)
        given = d_heads[:, h_cols].astype(BF16)
        d_weights = nt_dot(given, values).astype(BF16).astype(F32)
        dproj[:, v_cols] = tn_dot(weights, given).astype(BF16)
        inner = jnp.sum(d_weights * exact, -1, keepdims=True)
        d_scores = (exact * (d_weights - inner) * root).astype(BF16)
        d_queries = jnp.dot(d_scores, keys, preferred_element_type=F32)
        d_keys = tn_dot(d_scores, queries)
        dproj[:, q_cols] = normalise_back(d_queries, unit_q, inverse_q, qk_gain[0:1, :])
        dproj[:, k_cols] = normalise_back(d_keys, unit_k, inverse_k, qk_gain[1:2, :])

    for part in range(4):
        block = heads[...] if part == 0 else dproj[:, (part - 1) * half : part * half]
        parts_a[part, :, mine] = block.T

    def window(part, k, lines):
        cols = pl.ds(pl.multiple_of(((a + k) % 4) * rows, rows), rows)
        return parts_a.at[part, lines, cols]

    low, high, every = slice(0, 192), slice(192, 384), slice(0, 384)
    gathers = []
    for part in range(4):
        hops = [(0, every, 1), (0, every, 3), (3, low, 1), (1, high, 3)]
        refs = [(window(part, k, lines), at.along_a(to)) for k, lines, to in hops]
        gathers.append([remote(src, src, gs.at[part, i], gr.at[part, i], to) for i, (src, to) in enumerate(refs)])
    for part in range(4):
        gathers[part][0].start()
        gathers[part][1].start()

    def relay(part):
        for i in (0, 1):
            gathers[part][i].wait_recv()
            gathers[part][i + 2].start()

    def gathered(part):
        gathers[part][2].wait_recv()
        gathers[part][3].wait_recv()

    def held(part, i):
        return slice((3 * part + i) * half, (3 * part + i + 1) * half)

    def product(part, k):
        left = cot_a if part == 0 else normed_a
        cols = pl.ds(pl.multiple_of(((b + k) % 4) * half, half), half)
        return jnp.dot(parts_a[part], left[:, cols], preferred_element_type=F32)

    sums = []
    for part in range(4):
        far, after, ahead = (wo.at[held(part, i), :] for i in range(3))
        pairs = [
            (far.at[low, :], far_in.at[part, low, :], 1),
            (far.at[high, :], far_in.at[part, high, :], 3),
            (after, near_in.at[part, 0], 1),
            (ahead, near_in.at[part, 1], 3),
        ]
        sums.append([remote(src, dst, qs.at[part, i], qr.at[part, i], at.along_b(to)) for i, (src, dst, to) in enumerate(pairs)])

    def send_far(part):
        wo[held(part, 0), :] = product(part, 2).astype(BF16)
        sums[part][0].start()
        sums[part][1].start()

    def send_near(part):
        for i, k in enumerate((1, 3)):
            own_part[part] = product(part, k)
            sums[part][i].wait_recv()
            lines = (low, high)[i]
            own_part[part, lines, :] += far_in[part, lines, :].astype(F32)
            wo[held(part, 1 + i), :] = own_part[part].astype(BF16)
            sums[part][2 + i].start()
        own_part[part] = product(part, 0)

    def total_of(part):
        for i in (2, 3):
            sums[part][i].wait_recv()
        total = own_part[part] + near_in[part, 0].astype(F32) + near_in[part, 1].astype(F32)
        return (total * scale).T.astype(BF16)

    cots.finish()
    cot_far, cot_near = spread_ends(cot_full, cot_a, cs, cr, cl)
    for copy in cot_far:
        copy.wait_send()
    for copy in cot_near:
        copy.wait()

    sib_out, z_out = cot_full.at[0:4], cot_full.at[4:7]
    def attn_term(shard):
        rows = shard_rows(shard)
        return nt_dot(heads[...], wo[rows, :])

    def dn_term(shard):
        rows = shard_rows(shard)
        total = nt_dot(dproj[:, 0:half], wq[0, rows, :])
        total += nt_dot(dproj[:, half : 2 * half], wq[1, rows, :])
        return total + nt_dot(dproj[:, 2 * half : 3 * half], wq[2, rows, :])

    def to_sibling(term, out, into, send, recv):
        def step(k, carry):
            out[k] = term(((z + 1 + k) % 4) * 2 + 1 - c).astype(BF16)
            remote(out.at[k], into.at[k], send.at[k], recv.at[k], at.sibling()).start()
            return carry

        lax.fori_loop(0, 4, step, 0)

    def along_z(term, sib_o, sib, sib_send, sib_recv, out, into, send, recv, own):
        def step(k, carry):
            value = term(((z + 1 + k) % 4) * 2 + c)
            remote(sib_o.at[k], sib.at[k], sib_send.at[k], sib_recv.at[k], at.sibling()).wait()
            out[k] = (value + sib[k].astype(F32)).astype(BF16)
            remote(out.at[k], into.at[k], send.at[k], recv.at[k], at.along_z(1 + k)).start()
            return carry

        lax.fori_loop(0, 3, step, 0)
        value = term(z * 2 + c)
        remote(sib_o.at[3], sib.at[3], sib_send.at[3], sib_recv.at[3], at.sibling()).wait()
        own[...] = value + sib[3].astype(F32)

    to_sibling(attn_term, sib_out, sib_in, ss, sr)
    relay(0)
    to_sibling(dn_term, dn_sib_out, dn_sib_in, dss, dsr)
    relay(1)
    along_z(attn_term, sib_out, sib_in, ss, sr, z_out, z_in, zs, zr, own_at)
    for copy in cot_far:
        copy.wait_recv()
    gathered(0)
    send_far(0)
    relay(2)
    along_z(dn_term, dn_sib_out, dn_sib_in, dss, dsr, dn_z_out, dn_z_in, dzs, dzr, own_dn)
    relay(3)
    send_near(0)
    norms.finish()
    normed_far, normed_near = spread_ends(normed_full, normed_a, ns, nr, nl)
    for copy in normed_far + normed_near:
        copy.wait()
    for part in (1, 2, 3):
        gathered(part)
        send_far(part)
        if part > 1:
            send_near(part - 1)
    send_near(3)

    total = own_at[...]
    for k in range(3):
        remote(z_out.at[k], z_in.at[k], zs.at[k], zr.at[k], at.along_z(1 + k)).wait()
        total += z_in[k].astype(F32)
    output[...] = (packed[...].astype(F32) + total).astype(BF16)

    total = own_dn[...]
    for k in range(3):
        remote(dn_z_out.at[k], dn_z_in.at[k], dzs.at[k], dzr.at[k], at.along_z(1 + k)).wait()
        total += dn_z_in[k].astype(F32)
    rstd = columns[:, 1:2]
    unit = (packed[...].astype(F32) - columns[:, 0:1]) * rstd
    u = total * gain_part
    own_dn[...] = u
    ends = exchange(jnp.sum(u, -1, keepdims=True), jnp.sum(u * unit, -1, keepdims=True), en_out, en_in, ens, enr)
    for copy in ends:
        copy.start()
    for copy in ends:
        copy.wait()
    st_pad[0:8, :] = (en_out[...] + sum(en_in[k] for k in range(7))) * (1.0 / 6144.0)
    means = st_pad[...].T
    unit = (packed[...].astype(F32) - columns[:, 0:1]) * rstd
    grad = rstd * (own_dn[...] - means[:, 0:1] - unit * means[:, 1:2])
    input_grad[...] = (cot[...].astype(F32) + grad).astype(BF16)

    out_grad[...] = total_of(0)
    for t in range(3):
        qkv_grad[t] = total_of(1 + t)
    for part in range(4):
        for copy in gathers[part] + sums[part]:
            copy.wait_send()


def hand_over(*refs):
    sources, results, sem = refs[:4], refs[4:8], refs[8]
    copies = [pltpu.make_async_copy(src, dst, sem.at[i]) for i, (src, dst) in enumerate(zip(sources, results))]
    for copy in copies:
        copy.start()
    for copy in copies:
        copy.wait()


def shards(patches, dest_group, dest_row, segment, ln_gain, w_qkv, qk_gain, w_out, cotangent):
    vmem = pl.BlockSpec(memory_space=pltpu.VMEM)
    anywhere = pl.BlockSpec(memory_space=pl.ANY)
    dma = pltpu.SemaphoreType.DMA
    V = pltpu.VMEM
    scale = 1.0 / math.sqrt(4096)
    out_shape = (
        jax.ShapeDtypeStruct((256, 768), BF16),
        jax.ShapeDtypeStruct((256, 768), BF16),
        jax.ShapeDtypeStruct((3, 384, 384), BF16),
        jax.ShapeDtypeStruct((384, 384), BF16),
    )
    results = pl.pallas_call(
        functools.partial(whole, scale),
        out_shape=out_shape,
        in_specs=[vmem, vmem, vmem, vmem, vmem, anywhere, vmem, anywhere, vmem],
        out_specs=(vmem,) * 4,
        scratch_shapes=[
            V((512, 896), BF16), V((512, 896), BF16), V((256, 768), BF16),
            V((8, 256, 768), BF16), V((8, 256, 768), BF16),
            V((1024, 1536), BF16), V((1024, 1536), BF16), V((4, 384, 1024), BF16),
            V((3, 6144, 384), BF16), V((6144, 384), BF16),
            V((256, 1152), F32), V((256, 384), F32), V((256, 384), BF16), V((256, 1152), BF16),
            V((256, 128), F32), V((256, 128), F32), V((128, 256), F32),
            V((8, 256), F32), V((7, 8, 256), F32), V((8, 256), F32), V((7, 8, 256), F32),
            V((4, 256, 768), BF16), V((3, 256, 768), BF16),
            V((4, 256, 768), BF16), V((4, 256, 768), BF16), V((3, 256, 768), BF16), V((3, 256, 768), BF16),
            V((4, 384, 384), BF16), V((4, 2, 384, 384), BF16),
            V((4, 384, 384), F32), V((256, 768), F32), V((256, 768), F32),
            dma((2,)), dma((15,)), dma((15,)),
            dma((4,)), dma((4,)), dma((4,)), dma((4,)), dma((4,)), dma((4,)), dma((4,)), dma((4,)),
            dma((7,)), dma((7,)), dma((7,)), dma((7,)),
            dma((3, 4)), dma((3, 4)), dma((4,)), dma((3, 4)), dma((3, 4)), dma((4,)),
            dma((4, 4)), dma((4, 4)),
            dma((4,)), dma((4,)), dma((3,)), dma((3,)), dma((4,)), dma((4,)), dma((3,)), dma((3,)),
            dma((4, 4)), dma((4, 4)),
        ],
        compiler_params=pltpu.CompilerParams(
            collective_id=1, has_side_effects=True, vmem_limit_bytes=62 << 20
        ),
        name="whole",
    )(
        patches, dest_group.reshape(1, 256), dest_row.reshape(1, 256), segment.reshape(1, 256),
        ln_gain.reshape(1, 6144), jnp.transpose(w_qkv, (1, 0, 2)), qk_gain, w_out, cotangent,
    )
    output, input_grad, qkv_grad, out_grad = pl.pallas_call(
        hand_over,
        out_shape=out_shape,
        in_specs=[anywhere] * 4,
        out_specs=(anywhere,) * 4,
        scratch_shapes=[dma((4,))],
        name="hand_over",
    )(*results)
    return (output, input_grad, jnp.transpose(qkv_grad, (1, 0, 2)), out_grad)


def solution(mesh):
    placed = (
        P("dp", "mp"),
        P("dp"),
        P("dp"),
        P("dp"),
        P(),
        P(None, None, "mp"),
        P(),
        P(None, "mp"),
        P("dp", "mp"),
    )
    return jax.shard_map(
        shards,
        mesh=mesh,
        in_specs=placed,
        out_specs=(P("dp", "mp"), P("dp", "mp"), P("dp", None, "mp"), P("dp", "mp")),
        check_vma=False,
    )
```

```python
import functools
import math

import jax
import jax.numpy as jnp
from jax import lax
from jax.experimental import pallas as pl
from jax.experimental.pallas import tpu as pltpu
from jax.sharding import PartitionSpec as P

DH = 128
MESH = pl.DeviceIdType.MESH
F32 = jnp.float32
BF16 = jnp.bfloat16


class Place:
    def __init__(self):
        self.g, self.m = lax.axis_index("dp"), lax.axis_index("mp")
        self.x, self.y = self.g // 4, self.g % 4
        self.z, self.c = self.m // 2, self.m % 2
        c = self.c
        self.a = self.x * (1 - c) + self.y * c
        self.b = self.x * c + self.y * (1 - c)

    def along_a(self, k):
        x, y = (self.x + k * (1 - self.c)) % 4, (self.y + k * self.c) % 4
        return (x * 4 + y, self.m)

    def along_b(self, k):
        x, y = (self.x + k * self.c) % 4, (self.y + k * (1 - self.c)) % 4
        return (x * 4 + y, self.m)

    def along_z(self, k):
        return (self.g, ((self.z + k) % 4) * 2 + self.c)

    def along_m(self, k):
        return (self.g, (self.m + k) % 8)

    def over_xy(self, dx, dy):
        return (((self.x + dx) % 4) * 4 + (self.y + dy) % 4, self.m)

    def sibling(self):
        return (self.g, self.z * 2 + 1 - self.c)

    def block(self, q, j):
        c = self.c
        return 4 * (q * (1 - c) + j * c) + q * c + j * (1 - c)


def remote(src, dst, send, recv, device):
    return pltpu.make_async_remote_copy(
        src_ref=src, dst_ref=dst, send_sem=send, recv_sem=recv, device_id=device, device_id_type=MESH
    )


def nt_dot(left, right):
    return lax.dot_general(left, right, (((1,), (1,)), ((), ())), preferred_element_type=F32)


def tn_dot(left, right):
    return lax.dot_general(left, right, (((0,), (0,)), ((), ())), preferred_element_type=F32)


class Ring:
    def __init__(self, term, out, own, far_in, near_in, send, recv, along):
        size = own.shape[0]
        self.low, self.high = slice(0, size // 2), slice(size // 2, size)
        self.term, self.out, self.own, self.far_in, self.near_in = term, out, own, far_in, near_in
        pairs = [
            (out[0].at[self.low, :], far_in.at[self.low, :], 1),
            (out[0].at[self.high, :], far_in.at[self.high, :], 3),
            (out[1], near_in.at[0], 1),
            (out[2], near_in.at[1], 3),
        ]
        self.copies = [remote(src, dst, send.at[i], recv.at[i], along(to)) for i, (src, dst, to) in enumerate(pairs)]

    def send_far(self):
        self.out[0][...] = self.term(2).astype(BF16)
        self.copies[0].start()
        self.copies[1].start()

    def send_near(self):
        for i, k in enumerate((1, 3)):
            self.own[...] = self.term(k)
            self.copies[i].wait_recv()
            lines = (self.low, self.high)[i]
            self.own[lines, :] += self.far_in[lines, :].astype(F32)
            self.out[1 + i][...] = self.own[...].astype(BF16)
            self.copies[2 + i].start()
        self.own[...] = self.term(0)

    def total(self):
        self.copies[2].wait_recv()
        self.copies[3].wait_recv()
        return self.own[...] + self.near_in[0].astype(F32) + self.near_in[1].astype(F32)

    def finish(self):
        for copy in self.copies:
            copy.wait_send()


def whole(
    scale,
    patches_in, dest_group_in, dest_row_in, segment_in, gain_in, w_qkv, qk_gain_in, w_out, cot_in,
    output_to, input_grad_to, qkv_grad_to, out_grad_to,
    patches, dest_group, dest_row, segment, gain, qk_gain, cot, output, input_grad, qkv_grad, out_grad,
    outbox, inbox, packed, cot_full, normed_full, cot_a, normed_a, parts_a, wq, wo,
    proj, d_heads, heads, dproj, columns, places, st_pad, st_out, st_in, en_out, en_in,
    sib_in, z_in, dn_sib_out, dn_sib_in, dn_z_out, dn_z_in, far_in, near_in,
    own_part, own_at, own_dn,
    isem, osem, wsem, rs, rr, cz, czr, cb, cbr, nz, nzr, nb, nbr, sts, str_, ens, enr,
    cs, cr, cl, ns, nr, nl, gs, gr, ss, sr, zs, zr, dss, dsr, dzs, dzr, qs, qr,
):
    at = Place()
    a, b, c, z, m, g = at.a, at.b, at.c, at.z, at.m, at.g
    width, half, rows = 768, 384, 256
    load_wo = pltpu.make_async_copy(w_out, wo, wsem.at[0])
    load_wq = pltpu.make_async_copy(w_qkv, wq, wsem.at[1])
    pairs = [
        (dest_group_in, dest_group), (dest_row_in, dest_row), (segment_in, segment), (patches_in, patches),
        (cot_in, cot_full.at[m]), (cot_in, cot), (gain_in, gain), (qk_gain_in, qk_gain),
    ]
    loads = [pltpu.make_async_copy(src, dst, isem.at[i]) for i, (src, dst) in enumerate(pairs)]
    over_dp = [(dx, dy) for dx in range(4) for dy in range(4) if dx + dy > 0]
    barrier = pltpu.get_barrier_semaphore()
    met = [at.over_xy(dx, dy) for dx, dy in over_dp] + [at.along_m(k) for k in range(1, 8)]
    for device in met:
        pl.semaphore_signal(barrier, inc=1, device_id=device, device_id_type=MESH)
    for copy in loads + [load_wo, load_wq]:
        copy.start()
    for copy in loads[0:4]:
        copy.wait()

    group_row = dest_group[...]
    member = (lax.broadcasted_iota(jnp.int32, (16, rows), 0) == group_row).astype(F32)
    before = (
        lax.broadcasted_iota(jnp.int32, (rows, rows), 0) < lax.broadcasted_iota(jnp.int32, (rows, rows), 1)
    ).astype(BF16)
    rank = jnp.sum(jnp.dot(member.astype(BF16), before, preferred_element_type=F32) * member, 0, keepdims=True)
    slot = group_row.astype(F32) * 32.0 + rank
    pick = (lax.broadcasted_iota(jnp.int32, (512, rows), 0).astype(F32) == slot).astype(BF16)
    st_pad[...] = jnp.zeros_like(st_pad)
    st_pad[0:1, :] = dest_row[...].astype(F32) + 1.0
    st_pad[1:2, :] = segment[...].astype(F32)
    places[...] = st_pad[...].T
    address = jnp.broadcast_to(places[:, 0:1], (rows, 128)).astype(BF16)
    outbox[:, 0:width] = jnp.dot(pick, patches[...], preferred_element_type=F32).astype(BF16)
    outbox[:, width:] = jnp.dot(pick, address, preferred_element_type=F32).astype(BF16)
    for copy in loads[4:]:
        copy.wait()
    pl.semaphore_wait(barrier, len(met))

    here = pl.ds(pl.multiple_of(g * 32, 32), 32)
    routes = []
    for i, (dx, dy) in enumerate(over_dp):
        device = at.over_xy(dx, dy)
        there = pl.ds(pl.multiple_of(device[0] * 32, 32), 32)
        routes.append(remote(outbox.at[there, :], inbox.at[here, :], rs.at[i], rr.at[i], device))
    for copy in routes:
        copy.start()
    inbox[here, :] = outbox[here, :]

    class Collect:
        def __init__(self, full, z_send, z_recv, b_send, b_recv):
            up, down = at.along_z(1), at.along_z(3)
            self.z, self.b = [], []
            for h in (0, 1):
                part, low, high = (slice(128 * h + i, 128 * h + j) for i, j in ((0, 128), (0, 64), (64, 128)))
                own = full.at[m, part, :]
                hops = [(own, up), (own, down), (full.at[self.mine(1), low, :], up), (full.at[self.mine(3), high, :], down)]
                self.z.append([remote(src, src, z_send.at[h, i], z_recv.at[h, i], to) for i, (src, to) in enumerate(hops)])
                slabs = [full.at[self.mine(k), part, :] for k in range(4)]
                self.b.append([remote(slabs[k], slabs[k], b_send.at[h, k], b_recv.at[h, k], at.sibling()) for k in range(4)])

        def mine(self, k):
            return ((z + 4 - k) % 4) * 2 + c

        def others(self, k):
            return ((z + 4 - k) % 4) * 2 + 1 - c

        def start(self):
            for h in (0, 1):
                self.z[h][0].start()
                self.z[h][1].start()
                self.b[h][0].start()

        def near(self, h):
            for i in (0, 1):
                self.z[h][i].wait_recv()
                self.z[h][2 + i].start()
                self.b[h][1 + 2 * i].start()

        def far(self, h):
            self.z[h][2].wait_recv()
            self.z[h][3].wait_recv()
            self.b[h][2].start()

        def other(self, k, h):
            self.b[h][k].wait_recv()

        def finish(self):
            for copy in self.z[0] + self.z[1] + self.b[0] + self.b[1]:
                copy.wait_send()

    mine = pl.ds(pl.multiple_of(a * rows, rows), rows)

    def spread_slab(full, s, half_of, buf, send, recv, near):
        lines = pl.ds(pl.multiple_of(a * rows + 128 * half_of, 128), 128)
        for h in (0, 1):
            bx, by = (2 * s + h) // 4, (2 * s + h) % 4
            q, j = bx * (1 - c) + by * c, bx * c + by * (1 - c)
            k = (q - a + 4) % 4
            n = (k + 3) % 4
            src = full.at[s, 128 * half_of : 128 * half_of + 128, pl.ds(h * half, half)]
            dst = buf.at[lines, pl.ds(pl.multiple_of(j * half, half), half)]

            @pl.when(k == 0)
            def _():
                pltpu.make_async_copy(src, dst, near.at[half_of, j]).start()

            @pl.when(k != 0)
            def _():
                remote(src, dst, send.at[half_of, n, j], recv.at[half_of, n, j], at.along_a(k)).start()

    def spread_ends(full, buf, send, recv, near):
        src, dst = full.at[0, 0:128, 0:half], buf.at[0:128, 0:half]
        far = [
            remote(src, dst, send.at[h, k - 1, j], recv.at[h, k - 1, j], at.along_a(k))
            for h in (0, 1)
            for k in (1, 2, 3)
            for j in range(4)
        ]
        local = [pltpu.make_async_copy(src, dst, near.at[h, j]) for h in (0, 1) for j in range(4)]
        return far, local

    def shard_rows(s):
        return pl.ds(pl.multiple_of(s * width, width), width)

    cots = Collect(cot_full, cz, czr, cb, cbr)
    cots.start()
    load_wo.wait()

    def add_heads(s, first=False):
        term = jnp.dot(cot_full[s], wo[shard_rows(s), :], preferred_element_type=F32)
        d_heads[...] = term if first else d_heads[...] + term

    def spread_cot(s, h):
        spread_slab(cot_full, s, h, cot_a, cs, cr, cl)

    add_heads(m, True)
    cots.near(0)
    cots.other(0, 0)
    cots.other(0, 1)
    add_heads(cots.others(0))
    cots.near(1)
    cots.far(0)
    add_heads(cots.mine(1))
    add_heads(cots.mine(3))

    for copy in routes:
        copy.wait()
    arrived = inbox[:, width : width + 1].astype(F32)
    put = (lax.broadcasted_iota(jnp.int32, (512, rows), 1).astype(F32) + 1.0 == arrived).astype(BF16)
    block = tn_dot(put, inbox[:, 0:width])
    packed[...] = block.astype(BF16)

    def exchange(first, second, out, into, send, recv):
        lane = lax.broadcasted_iota(jnp.int32, (rows, 128), 1)
        out[...] = jnp.where(lane == 0, first, jnp.where(lane == 1, second, 0.0)).T[0:8]
        return [remote(out, into.at[k - 1], send.at[k - 1], recv.at[k - 1], at.along_m(k)) for k in range(1, 8)]

    part_mean = jnp.mean(block, -1, keepdims=True)
    part_center = block - part_mean
    stats = exchange(part_mean, jnp.sum(part_center * part_center, -1, keepdims=True), st_out, st_in, sts, str_)
    for copy in stats:
        copy.start()

    for h in (0, 1):
        spread_cot(m, h)
        spread_cot(cots.others(0), h)
        for k in (1, 3):
            spread_cot(cots.mine(k), h)
            cots.other(k, h)
            spread_cot(cots.others(k), h)
    spread_cot(cots.mine(2), 0)
    for copy in stats:
        copy.wait()
    parts = [st_out[...]] + [st_in[k] for k in range(7)]
    mean = sum(part[0:1] for part in parts) * 0.125
    spread = sum(part[1:2] + width * (part[0:1] - mean) * (part[0:1] - mean) for part in parts)
    st_pad[0:1, :] = mean
    st_pad[1:2, :] = lax.rsqrt(spread * (1.0 / 6144.0) + 1e-06)
    columns[...] = st_pad[...].T
    gain_part = gain[:, pl.ds(pl.multiple_of(m * width, width), width)]
    unit = (packed[...].astype(F32) - columns[:, 0:1]) * columns[:, 1:2]
    normed_full[m] = (unit * gain_part).astype(BF16)
    norms = Collect(normed_full, nz, nzr, nb, nbr)
    norms.start()

    def spread_normed(s, h):
        spread_slab(normed_full, s, h, normed_a, ns, nr, nl)

    def add_projected(s, first=False):
        for t in range(3):
            cols = slice(t * half, (t + 1) * half)
            term = jnp.dot(normed_full[s], wq[t, shard_rows(s), :], preferred_element_type=F32)
            proj[:, cols] = term if first else proj[:, cols] + term

    cots.far(1)
    spread_cot(cots.mine(2), 1)
    for h in (0, 1):
        cots.other(2, h)
        spread_cot(cots.others(2), h)
    for h in (0, 1):
        spread_normed(m, h)
    norms.near(0)
    for k in (1, 3):
        spread_normed(norms.mine(k), 0)
    for h in (0, 1):
        norms.other(0, h)
        spread_normed(norms.others(0), h)
    load_wq.wait()
    add_projected(m, True)
    add_projected(norms.others(0))
    for k in (1, 3):
        norms.other(k, 0)
        spread_normed(norms.others(k), 0)
    for s in (cots.others(1), cots.others(3), cots.mine(2), cots.others(2)):
        add_heads(s)
    norms.near(1)
    norms.far(0)
    spread_normed(norms.mine(2), 0)
    for k in (1, 3):
        spread_normed(norms.mine(k), 1)
        add_projected(norms.mine(k))
    norms.other(2, 0)
    spread_normed(norms.others(2), 0)
    for k in (1, 3):
        norms.other(k, 1)
        spread_normed(norms.others(k), 1)
    for k in (1, 3):
        add_projected(norms.others(k))
    norms.far(1)
    spread_normed(norms.mine(2), 1)
    norms.other(2, 1)
    spread_normed(norms.others(2), 1)
    add_projected(norms.mine(2))
    add_projected(norms.others(2))
    same = places[:, 1:2] == segment[...].astype(F32)

    def normalise(values):
        center = values - jnp.mean(values, -1, keepdims=True)
        inverse = lax.rsqrt(jnp.mean(center * center, -1, keepdims=True) + 1e-06)
        return center * inverse, inverse

    def normalise_back(grad, unit, inverse, weight):
        scaled = grad.astype(BF16).astype(F32) * weight
        inner = scaled - jnp.mean(scaled, -1, keepdims=True) - unit * jnp.mean(scaled * unit, -1, keepdims=True)
        return (inverse * inner).astype(BF16)

    root = DH ** (-0.5)
    for h in range(3):
        q_cols, k_cols, v_cols = (slice(t * half + h * DH, t * half + (h + 1) * DH) for t in range(3))
        h_cols = slice(h * DH, (h + 1) * DH)
        unit_q, inverse_q = normalise(proj[:, q_cols])
        unit_k, inverse_k = normalise(proj[:, k_cols])
        queries = (unit_q * qk_gain[0:1, :]).astype(BF16)
        keys = (unit_k * qk_gain[1:2, :]).astype(BF16)
        values = proj[:, v_cols].astype(BF16)
        raised = jnp.where(same, jnp.exp(nt_dot(queries, keys) * root), 0.0)
        exact = raised / jnp.sum(raised, -1, keepdims=True)
        weights = exact.astype(BF16)
        heads[:, h_cols] = jnp.dot(weights, values, preferred_element_type=F32).astype(BF16)
        given = d_heads[:, h_cols].astype(BF16)
        d_weights = nt_dot(given, values).astype(BF16).astype(F32)
        dproj[:, v_cols] = tn_dot(weights, given).astype(BF16)
        inner = jnp.sum(d_weights * exact, -1, keepdims=True)
        d_scores = (exact * (d_weights - inner) * root).astype(BF16)
        d_queries = jnp.dot(d_scores, keys, preferred_element_type=F32)
        d_keys = tn_dot(d_scores, queries)
        dproj[:, q_cols] = normalise_back(d_queries, unit_q, inverse_q, qk_gain[0:1, :])
        dproj[:, k_cols] = normalise_back(d_keys, unit_k, inverse_k, qk_gain[1:2, :])

    for part in range(4):
        block = heads[...] if part == 0 else dproj[:, (part - 1) * half : part * half]
        parts_a[part, :, mine] = block.T

    def window(part, k, lines):
        cols = pl.ds(pl.multiple_of(((a + k) % 4) * rows, rows), rows)
        return parts_a.at[part, lines, cols]

    low, high, every = slice(0, 192), slice(192, 384), slice(0, 384)
    gathers = []
    for part in range(4):
        hops = [(0, every, 1), (0, every, 3), (3, low, 1), (1, high, 3)]
        refs = [(window(part, k, lines), at.along_a(to)) for k, lines, to in hops]
        gathers.append([remote(src, src, gs.at[part, i], gr.at[part, i], to) for i, (src, to) in enumerate(refs)])
    for part in range(4):
        gathers[part][0].start()
        gathers[part][1].start()

    def relay(part):
        for i in (0, 1):
            gathers[part][i].wait_recv()
            gathers[part][i + 2].start()

    def gathered(part):
        gathers[part][2].wait_recv()
        gathers[part][3].wait_recv()

    def held(part, i):
        return slice((3 * part + i) * half, (3 * part + i + 1) * half)

    def product(part, k):
        left = cot_a if part == 0 else normed_a
        cols = pl.ds(pl.multiple_of(((b + k) % 4) * half, half), half)
        return jnp.dot(parts_a[part], left[:, cols], preferred_element_type=F32)

    sums = []
    for part in range(4):
        out = [wo.at[held(part, i), :] for i in range(3)]
        sums.append(
            Ring(
                functools.partial(product, part), out, own_part.at[part], far_in.at[part], near_in.at[part],
                qs.at[part], qr.at[part], at.along_b,
            )
        )

    cots.finish()
    cot_far, cot_near = spread_ends(cot_full, cot_a, cs, cr, cl)
    for copy in cot_far:
        copy.wait_send()
    for copy in cot_near:
        copy.wait()

    def attn_term(shard):
        return nt_dot(heads[...], wo[shard_rows(shard), :])

    def dn_term(shard):
        total = nt_dot(dproj[:, 0:half], wq[0, shard_rows(shard), :])
        total += nt_dot(dproj[:, half : 2 * half], wq[1, shard_rows(shard), :])
        return total + nt_dot(dproj[:, 2 * half : 3 * half], wq[2, shard_rows(shard), :])

    class ChipSum:
        def __init__(self, term, out, into, send, recv):
            self.term, self.out, self.into = term, out, into
            self.copies = [remote(out.at[k], into.at[k], send.at[k], recv.at[k], at.sibling()) for k in range(4)]

        def start(self):
            for k in (2, 1, 3, 0):
                self.out[k] = self.term(((z + k) % 4) * 2 + 1 - c).astype(BF16)
                self.copies[k].start()

        def sum(self, k):
            value = self.term(((z + k) % 4) * 2 + c)
            self.copies[k].wait()
            return value + self.into[k].astype(F32)

    attn_chip = ChipSum(attn_term, cot_full.at[0:4], sib_in, ss, sr)
    dn_chip = ChipSum(dn_term, dn_sib_out, dn_sib_in, dss, dsr)
    attn_out = [cot_full.at[4 + i] for i in range(3)]
    dn_out = [dn_z_out.at[i] for i in range(3)]
    attn_ring = Ring(attn_chip.sum, attn_out, own_at, z_in.at[0], z_in.at[1:3], zs, zr, at.along_z)
    dn_ring = Ring(dn_chip.sum, dn_out, own_dn, dn_z_in.at[0], dn_z_in.at[1:3], dzs, dzr, at.along_z)

    attn_chip.start()
    dn_chip.start()
    attn_ring.send_far()
    attn_ring.send_near()
    dn_ring.send_far()
    relay(0)
    relay(1)
    dn_ring.send_near()
    relay(2)
    relay(3)
    for copy in cot_far:
        copy.wait_recv()
    gathered(0)
    sums[0].send_far()
    norms.finish()
    normed_far, normed_near = spread_ends(normed_full, normed_a, ns, nr, nl)
    for copy in normed_far + normed_near:
        copy.wait()
    for part in (1, 2, 3):
        gathered(part)
        sums[part].send_far()
        sums[part - 1].send_near()
    sums[3].send_near()

    stores = [pltpu.make_async_copy(output, output_to, osem.at[0]), pltpu.make_async_copy(input_grad, input_grad_to, osem.at[1])]
    stores.append(pltpu.make_async_copy(out_grad, out_grad_to, osem.at[2]))
    stores += [pltpu.make_async_copy(qkv_grad.at[t], qkv_grad_to.at[t], osem.at[3 + t]) for t in range(3)]
    output[...] = (packed[...].astype(F32) + attn_ring.total()).astype(BF16)
    stores[0].start()
    total = dn_ring.total()
    rstd = columns[:, 1:2]
    unit = (packed[...].astype(F32) - columns[:, 0:1]) * rstd
    u = total * gain_part
    own_dn[...] = u
    ends = exchange(jnp.sum(u, -1, keepdims=True), jnp.sum(u * unit, -1, keepdims=True), en_out, en_in, ens, enr)
    for copy in ends:
        copy.start()
    for copy in ends:
        copy.wait()
    st_pad[0:8, :] = (en_out[...] + sum(en_in[k] for k in range(7))) * (1.0 / 6144.0)
    means = st_pad[...].T
    unit = (packed[...].astype(F32) - columns[:, 0:1]) * rstd
    grad = rstd * (own_dn[...] - means[:, 0:1] - unit * means[:, 1:2])
    input_grad[...] = (cot[...].astype(F32) + grad).astype(BF16)
    stores[1].start()
    for part in range(4):
        result = (sums[part].total() * scale).T.astype(BF16)
        if part == 0:
            out_grad[...] = result
        else:
            qkv_grad[part - 1] = result
        stores[2 + part].start()
    for ring in sums + [attn_ring, dn_ring]:
        ring.finish()
    for part in range(4):
        for copy in gathers[part]:
            copy.wait_send()
    for copy in stores:
        copy.wait()


def hand_over(*refs):
    sources, results, held, came, went = refs[:4], refs[4:8], refs[8:12], refs[12], refs[13]
    ins = [pltpu.make_async_copy(src, buf, came.at[i]) for i, (src, buf) in enumerate(zip(sources, held))]
    outs = [pltpu.make_async_copy(buf, dst, went.at[i]) for i, (buf, dst) in enumerate(zip(held, results))]
    for copy in ins:
        copy.start()
    for before, after in zip(ins, outs):
        before.wait()
        after.start()
    for copy in outs:
        copy.wait()


def shards(patches, dest_group, dest_row, segment, ln_gain, w_qkv, qk_gain, w_out, cotangent):
    anywhere = pl.BlockSpec(memory_space=pl.ANY)
    dma = pltpu.SemaphoreType.DMA
    V = pltpu.VMEM
    scale = 1.0 / math.sqrt(4096)
    out_shape = (
        jax.ShapeDtypeStruct((256, 768), BF16),
        jax.ShapeDtypeStruct((256, 768), BF16),
        jax.ShapeDtypeStruct((3, 384, 384), BF16),
        jax.ShapeDtypeStruct((384, 384), BF16),
    )
    results = pl.pallas_call(
        functools.partial(whole, scale),
        out_shape=out_shape,
        in_specs=[anywhere] * 9,
        out_specs=(anywhere,) * 4,
        scratch_shapes=[
            V((256, 768), BF16), V((1, 256), jnp.int32), V((1, 256), jnp.int32), V((1, 256), jnp.int32),
            V((1, 6144), F32), V((2, 128), F32), V((256, 768), BF16),
            *(V(shape.shape, BF16) for shape in out_shape),
            V((512, 896), BF16), V((512, 896), BF16), V((256, 768), BF16),
            V((8, 256, 768), BF16), V((8, 256, 768), BF16),
            V((1024, 1536), BF16), V((1024, 1536), BF16), V((4, 384, 1024), BF16),
            V((3, 6144, 384), BF16), V((6144, 384), BF16),
            V((256, 1152), F32), V((256, 384), F32), V((256, 384), BF16), V((256, 1152), BF16),
            V((256, 128), F32), V((256, 128), F32), V((128, 256), F32),
            V((8, 256), F32), V((7, 8, 256), F32), V((8, 256), F32), V((7, 8, 256), F32),
            V((4, 256, 768), BF16), V((3, 256, 768), BF16),
            V((4, 256, 768), BF16), V((4, 256, 768), BF16), V((3, 256, 768), BF16), V((3, 256, 768), BF16),
            V((4, 384, 384), BF16), V((4, 2, 384, 384), BF16),
            V((4, 384, 384), F32), V((256, 768), F32), V((256, 768), F32),
            dma((8,)), dma((6,)), dma((2,)), dma((15,)), dma((15,)),
            dma((2, 4)), dma((2, 4)), dma((2, 4)), dma((2, 4)), dma((2, 4)), dma((2, 4)), dma((2, 4)), dma((2, 4)),
            dma((7,)), dma((7,)), dma((7,)), dma((7,)),
            dma((2, 3, 4)), dma((2, 3, 4)), dma((2, 4)), dma((2, 3, 4)), dma((2, 3, 4)), dma((2, 4)),
            dma((4, 4)), dma((4, 4)),
            dma((4,)), dma((4,)), dma((4,)), dma((4,)), dma((4,)), dma((4,)), dma((4,)), dma((4,)),
            dma((4, 4)), dma((4, 4)),
        ],
        compiler_params=pltpu.CompilerParams(
            collective_id=1, has_side_effects=True, vmem_limit_bytes=62 << 20
        ),
        name="whole",
    )(
        patches, dest_group.reshape(1, 256), dest_row.reshape(1, 256), segment.reshape(1, 256),
        ln_gain.reshape(1, 6144), jnp.transpose(w_qkv, (1, 0, 2)), qk_gain, w_out, cotangent,
    )
    output, input_grad, qkv_grad, out_grad = pl.pallas_call(
        hand_over,
        out_shape=out_shape,
        in_specs=[anywhere] * 4,
        out_specs=(anywhere,) * 4,
        scratch_shapes=[V(shape.shape, BF16) for shape in out_shape] + [dma((4,)), dma((4,))],
        name="hand_over",
    )(*results)
    return (output, input_grad, jnp.transpose(qkv_grad, (1, 0, 2)), out_grad)


def solution(mesh):
    placed = (
        P("dp", "mp"),
        P("dp"),
        P("dp"),
        P("dp"),
        P(),
        P(None, None, "mp"),
        P(),
        P(None, "mp"),
        P("dp", "mp"),
    )
    return jax.shard_map(
        shards,
        mesh=mesh,
        in_specs=placed,
        out_specs=(P("dp", "mp"), P("dp", "mp"), P("dp", None, "mp"), P("dp", "mp")),
        check_vma=False,
    )
```

```python
import functools
import math

import jax
import jax.numpy as jnp
from jax import lax
from jax.experimental import pallas as pl
from jax.experimental.pallas import tpu as pltpu
from jax.sharding import PartitionSpec as P

DH = 128
MESH = pl.DeviceIdType.MESH
F32 = jnp.float32
BF16 = jnp.bfloat16


class Place:
    def __init__(self):
        self.g, self.m = lax.axis_index("dp"), lax.axis_index("mp")
        self.x, self.y = self.g // 4, self.g % 4
        self.z, self.c = self.m // 2, self.m % 2
        c = self.c
        self.a = self.x * (1 - c) + self.y * c
        self.b = self.x * c + self.y * (1 - c)

    def along_a(self, k):
        x, y = (self.x + k * (1 - self.c)) % 4, (self.y + k * self.c) % 4
        return (x * 4 + y, self.m)

    def along_b(self, k):
        x, y = (self.x + k * self.c) % 4, (self.y + k * (1 - self.c)) % 4
        return (x * 4 + y, self.m)

    def along_z(self, k):
        return (self.g, ((self.z + k) % 4) * 2 + self.c)

    def along_m(self, k):
        return (self.g, (self.m + k) % 8)

    def over_xy(self, dx, dy):
        return (((self.x + dx) % 4) * 4 + (self.y + dy) % 4, self.m)

    def sibling(self):
        return (self.g, self.z * 2 + 1 - self.c)

    def block(self, q, j):
        c = self.c
        return 4 * (q * (1 - c) + j * c) + q * c + j * (1 - c)


def remote(src, dst, send, recv, device):
    return pltpu.make_async_remote_copy(
        src_ref=src, dst_ref=dst, send_sem=send, recv_sem=recv, device_id=device, device_id_type=MESH
    )


def nt_dot(left, right):
    return lax.dot_general(left, right, (((1,), (1,)), ((), ())), preferred_element_type=F32)


def tn_dot(left, right):
    return lax.dot_general(left, right, (((0,), (0,)), ((), ())), preferred_element_type=F32)


class Ring:
    def __init__(self, term, out, own, far_in, near_in, send, recv, along):
        size = own.shape[0]
        self.low, self.high = slice(0, size // 2), slice(size // 2, size)
        self.term, self.out, self.own, self.far_in, self.near_in = term, out, own, far_in, near_in
        pairs = [
            (out[0].at[self.low, :], far_in.at[self.low, :], 1),
            (out[0].at[self.high, :], far_in.at[self.high, :], 3),
            (out[1], near_in.at[0], 1),
            (out[2], near_in.at[1], 3),
        ]
        self.copies = [remote(src, dst, send.at[i], recv.at[i], along(to)) for i, (src, dst, to) in enumerate(pairs)]

    def send_far(self):
        self.out[0][...] = self.term(2).astype(BF16)
        self.copies[0].start()
        self.copies[1].start()

    def send_near(self):
        for i, k in enumerate((1, 3)):
            self.own[...] = self.term(k)
            self.copies[i].wait_recv()
            lines = (self.low, self.high)[i]
            self.own[lines, :] += self.far_in[lines, :].astype(F32)
            self.out[1 + i][...] = self.own[...].astype(BF16)
            self.copies[2 + i].start()
        self.own[...] = self.term(0)

    def total(self):
        self.copies[2].wait_recv()
        self.copies[3].wait_recv()
        return self.own[...] + self.near_in[0].astype(F32) + self.near_in[1].astype(F32)

    def finish(self):
        for copy in self.copies:
            copy.wait_send()


def whole(
    scale,
    patches_in, dest_group_in, dest_row_in, segment_in, gain_in, w_qkv, qk_gain_in, w_out, cot_in,
    output_to, input_grad_to, qkv_grad_to, out_grad_to,
    patches, dest_group, dest_row, segment, gain, qk_gain, cot, output, input_grad, qkv_grad, out_grad,
    outbox, inbox, packed, cot_full, normed_full, cot_a, normed_a, parts_a, wq, wo,
    proj, d_heads, heads, dproj, columns, places, st_pad, st_out, st_in, en_out, en_in,
    sib_out, sib_in, z_out, z_in, dn_sib_out, dn_sib_in, dn_z_out, dn_z_in, far_in, near_in,
    own_part, own_at, own_dn,
    isem, osem, wsem, rs, rr, cz, czr, cb, cbr, nz, nzr, nb, nbr, sts, str_, ens, enr,
    cs, cr, cl, ns, nr, nl, gs, gr, ss, sr, zs, zr, dss, dsr, dzs, dzr, qs, qr,
):
    at = Place()
    a, b, c, z, m, g = at.a, at.b, at.c, at.z, at.m, at.g
    width, half, rows = 768, 384, 256
    load_wo = pltpu.make_async_copy(w_out, wo, wsem.at[0])
    load_wq = pltpu.make_async_copy(w_qkv, wq, wsem.at[1])
    pairs = [
        (dest_group_in, dest_group), (dest_row_in, dest_row), (segment_in, segment), (patches_in, patches),
        (cot_in, cot_full.at[m]), (cot_in, cot), (gain_in, gain), (qk_gain_in, qk_gain),
    ]
    loads = [pltpu.make_async_copy(src, dst, isem.at[i]) for i, (src, dst) in enumerate(pairs)]
    over_dp = [(dx, dy) for dx in range(4) for dy in range(4) if dx + dy > 0]
    barrier = pltpu.get_barrier_semaphore()
    met = [at.over_xy(dx, dy) for dx, dy in over_dp] + [at.along_m(k) for k in range(1, 8)]
    for device in met:
        pl.semaphore_signal(barrier, inc=1, device_id=device, device_id_type=MESH)
    for copy in loads + [load_wo, load_wq]:
        copy.start()
    for copy in loads[0:4]:
        copy.wait()

    group_row = dest_group[...]
    member = (lax.broadcasted_iota(jnp.int32, (16, rows), 0) == group_row).astype(F32)
    before = (
        lax.broadcasted_iota(jnp.int32, (rows, rows), 0) < lax.broadcasted_iota(jnp.int32, (rows, rows), 1)
    ).astype(BF16)
    rank = jnp.sum(jnp.dot(member.astype(BF16), before, preferred_element_type=F32) * member, 0, keepdims=True)
    slot = group_row.astype(F32) * 32.0 + rank
    pick = (lax.broadcasted_iota(jnp.int32, (512, rows), 0).astype(F32) == slot).astype(BF16)
    st_pad[...] = jnp.zeros_like(st_pad)
    st_pad[0:1, :] = dest_row[...].astype(F32) + 1.0
    st_pad[1:2, :] = segment[...].astype(F32)
    places[...] = st_pad[...].T
    address = jnp.broadcast_to(places[:, 0:1], (rows, 128)).astype(BF16)
    outbox[:, 0:width] = jnp.dot(pick, patches[...], preferred_element_type=F32).astype(BF16)
    outbox[:, width:] = jnp.dot(pick, address, preferred_element_type=F32).astype(BF16)
    for copy in loads[4:]:
        copy.wait()
    pl.semaphore_wait(barrier, len(met))

    here = pl.ds(pl.multiple_of(g * 32, 32), 32)
    routes = []
    for i, (dx, dy) in enumerate(over_dp):
        device = at.over_xy(dx, dy)
        there = pl.ds(pl.multiple_of(device[0] * 32, 32), 32)
        routes.append(remote(outbox.at[there, :], inbox.at[here, :], rs.at[i], rr.at[i], device))
    for copy in routes:
        copy.start()
    inbox[here, :] = outbox[here, :]

    class Collect:
        def __init__(self, full, z_send, z_recv, b_send, b_recv):
            up, down = at.along_z(1), at.along_z(3)
            self.z, self.b = [], []
            for h in (0, 1):
                part, low, high = (slice(128 * h + i, 128 * h + j) for i, j in ((0, 128), (0, 64), (64, 128)))
                own = full.at[m, part, :]
                hops = [(own, up), (own, down), (full.at[self.mine(1), low, :], up), (full.at[self.mine(3), high, :], down)]
                self.z.append([remote(src, src, z_send.at[h, i], z_recv.at[h, i], to) for i, (src, to) in enumerate(hops)])
                slabs = [full.at[self.mine(k), part, :] for k in range(4)]
                self.b.append([remote(slabs[k], slabs[k], b_send.at[h, k], b_recv.at[h, k], at.sibling()) for k in range(4)])

        def mine(self, k):
            return ((z + 4 - k) % 4) * 2 + c

        def others(self, k):
            return ((z + 4 - k) % 4) * 2 + 1 - c

        def start(self):
            for h in (0, 1):
                self.z[h][0].start()
                self.z[h][1].start()
                self.b[h][0].start()

        def near(self, h):
            for i in (0, 1):
                self.z[h][i].wait_recv()
                self.z[h][2 + i].start()
                self.b[h][1 + 2 * i].start()

        def far(self, h):
            self.z[h][2].wait_recv()
            self.z[h][3].wait_recv()
            self.b[h][2].start()

        def other(self, k, h):
            self.b[h][k].wait_recv()

        def finish(self):
            for copy in self.z[0] + self.z[1] + self.b[0] + self.b[1]:
                copy.wait_send()

    mine = pl.ds(pl.multiple_of(a * rows, rows), rows)

    def spread_slab(full, s, half_of, buf, send, recv, near):
        lines = pl.ds(pl.multiple_of(a * rows + 128 * half_of, 128), 128)
        for h in (0, 1):
            bx, by = (2 * s + h) // 4, (2 * s + h) % 4
            q, j = bx * (1 - c) + by * c, bx * c + by * (1 - c)
            k = (q - a + 4) % 4
            n = (k + 3) % 4
            src = full.at[s, 128 * half_of : 128 * half_of + 128, pl.ds(h * half, half)]
            dst = buf.at[lines, pl.ds(pl.multiple_of(j * half, half), half)]

            @pl.when(k == 0)
            def _():
                pltpu.make_async_copy(src, dst, near.at[half_of, j]).start()

            @pl.when(k != 0)
            def _():
                remote(src, dst, send.at[half_of, n, j], recv.at[half_of, n, j], at.along_a(k)).start()

    def spread_ends(full, buf, send, recv, near):
        src, dst = full.at[0, 0:128, 0:half], buf.at[0:128, 0:half]
        far = [
            remote(src, dst, send.at[h, k - 1, j], recv.at[h, k - 1, j], at.along_a(k))
            for h in (0, 1)
            for k in (1, 2, 3)
            for j in range(4)
        ]
        local = [pltpu.make_async_copy(src, dst, near.at[h, j]) for h in (0, 1) for j in range(4)]
        return far, local

    def shard_rows(s):
        return pl.ds(pl.multiple_of(s * width, width), width)

    cots = Collect(cot_full, cz, czr, cb, cbr)
    cots.start()
    load_wo.wait()

    def add_heads(s, first=False):
        term = jnp.dot(cot_full[s], wo[shard_rows(s), :], preferred_element_type=F32)
        d_heads[...] = term if first else d_heads[...] + term

    def spread_cot(s, h):
        spread_slab(cot_full, s, h, cot_a, cs, cr, cl)

    add_heads(m, True)
    cots.near(0)
    cots.other(0, 0)
    cots.other(0, 1)
    add_heads(cots.others(0))
    cots.near(1)
    cots.far(0)
    add_heads(cots.mine(1))
    add_heads(cots.mine(3))

    for copy in routes:
        copy.wait()
    arrived = inbox[:, width : width + 1].astype(F32)
    put = (lax.broadcasted_iota(jnp.int32, (512, rows), 1).astype(F32) + 1.0 == arrived).astype(BF16)
    block = tn_dot(put, inbox[:, 0:width])
    packed[...] = block.astype(BF16)

    def exchange(first, second, out, into, send, recv):
        lane = lax.broadcasted_iota(jnp.int32, (rows, 128), 1)
        out[...] = jnp.where(lane == 0, first, jnp.where(lane == 1, second, 0.0)).T[0:8]
        return [remote(out, into.at[k - 1], send.at[k - 1], recv.at[k - 1], at.along_m(k)) for k in range(1, 8)]

    part_mean = jnp.mean(block, -1, keepdims=True)
    part_center = block - part_mean
    stats = exchange(part_mean, jnp.sum(part_center * part_center, -1, keepdims=True), st_out, st_in, sts, str_)
    for copy in stats:
        copy.start()

    for h in (0, 1):
        spread_cot(m, h)
        spread_cot(cots.others(0), h)
        for k in (1, 3):
            spread_cot(cots.mine(k), h)
            cots.other(k, h)
            spread_cot(cots.others(k), h)
    spread_cot(cots.mine(2), 0)
    for copy in stats:
        copy.wait()
    parts = [st_out[...]] + [st_in[k] for k in range(7)]
    mean = sum(part[0:1] for part in parts) * 0.125
    spread = sum(part[1:2] + width * (part[0:1] - mean) * (part[0:1] - mean) for part in parts)
    st_pad[0:1, :] = mean
    st_pad[1:2, :] = lax.rsqrt(spread * (1.0 / 6144.0) + 1e-06)
    columns[...] = st_pad[...].T
    gain_part = gain[:, pl.ds(pl.multiple_of(m * width, width), width)]
    unit = (packed[...].astype(F32) - columns[:, 0:1]) * columns[:, 1:2]
    normed_full[m] = (unit * gain_part).astype(BF16)
    norms = Collect(normed_full, nz, nzr, nb, nbr)
    norms.start()

    def spread_normed(s, h):
        spread_slab(normed_full, s, h, normed_a, ns, nr, nl)

    def add_projected(s, first=False):
        for t in range(3):
            cols = slice(t * half, (t + 1) * half)
            term = jnp.dot(normed_full[s], wq[t, shard_rows(s), :], preferred_element_type=F32)
            proj[:, cols] = term if first else proj[:, cols] + term

    cots.far(1)
    spread_cot(cots.mine(2), 1)
    for h in (0, 1):
        cots.other(2, h)
        spread_cot(cots.others(2), h)
    for h in (0, 1):
        spread_normed(m, h)
    norms.near(0)
    for k in (1, 3):
        spread_normed(norms.mine(k), 0)
    for h in (0, 1):
        norms.other(0, h)
        spread_normed(norms.others(0), h)
    load_wq.wait()
    add_projected(m, True)
    add_projected(norms.others(0))
    for k in (1, 3):
        norms.other(k, 0)
        spread_normed(norms.others(k), 0)
    for s in (cots.others(1), cots.others(3), cots.mine(2), cots.others(2)):
        add_heads(s)
    norms.near(1)
    norms.far(0)
    spread_normed(norms.mine(2), 0)
    for k in (1, 3):
        spread_normed(norms.mine(k), 1)
        add_projected(norms.mine(k))
    norms.other(2, 0)
    spread_normed(norms.others(2), 0)
    for k in (1, 3):
        norms.other(k, 1)
        spread_normed(norms.others(k), 1)
    for k in (1, 3):
        add_projected(norms.others(k))
    norms.far(1)
    spread_normed(norms.mine(2), 1)
    norms.other(2, 1)
    spread_normed(norms.others(2), 1)
    add_projected(norms.mine(2))
    add_projected(norms.others(2))
    same = places[:, 1:2] == segment[...].astype(F32)

    def normalise(values):
        center = values - jnp.mean(values, -1, keepdims=True)
        inverse = lax.rsqrt(jnp.mean(center * center, -1, keepdims=True) + 1e-06)
        return center * inverse, inverse

    def normalise_back(grad, unit, inverse, weight):
        scaled = grad.astype(BF16).astype(F32) * weight
        inner = scaled - jnp.mean(scaled, -1, keepdims=True) - unit * jnp.mean(scaled * unit, -1, keepdims=True)
        return (inverse * inner).astype(BF16)

    root = DH ** (-0.5)
    for h in range(3):
        q_cols, k_cols, v_cols = (slice(t * half + h * DH, t * half + (h + 1) * DH) for t in range(3))
        h_cols = slice(h * DH, (h + 1) * DH)
        unit_q, inverse_q = normalise(proj[:, q_cols])
        unit_k, inverse_k = normalise(proj[:, k_cols])
        queries = (unit_q * qk_gain[0:1, :]).astype(BF16)
        keys = (unit_k * qk_gain[1:2, :]).astype(BF16)
        values = proj[:, v_cols].astype(BF16)
        raised = jnp.where(same, jnp.exp(nt_dot(queries, keys) * root), 0.0)
        exact = raised / jnp.sum(raised, -1, keepdims=True)
        weights = exact.astype(BF16)
        heads[:, h_cols] = jnp.dot(weights, values, preferred_element_type=F32).astype(BF16)
        given = d_heads[:, h_cols].astype(BF16)
        d_weights = nt_dot(given, values).astype(BF16).astype(F32)
        dproj[:, v_cols] = tn_dot(weights, given).astype(BF16)
        inner = jnp.sum(d_weights * exact, -1, keepdims=True)
        d_scores = (exact * (d_weights - inner) * root).astype(BF16)
        d_queries = jnp.dot(d_scores, keys, preferred_element_type=F32)
        d_keys = tn_dot(d_scores, queries)
        dproj[:, q_cols] = normalise_back(d_queries, unit_q, inverse_q, qk_gain[0:1, :])
        dproj[:, k_cols] = normalise_back(d_keys, unit_k, inverse_k, qk_gain[1:2, :])

    for part in range(4):
        block = heads[...] if part == 0 else dproj[:, (part - 1) * half : part * half]
        parts_a[part, :, mine] = block.T

    def window(part, k, lines):
        cols = pl.ds(pl.multiple_of(((a + k) % 4) * rows, rows), rows)
        return parts_a.at[part, lines, cols]

    low, high, every = slice(0, 192), slice(192, 384), slice(0, 384)
    gathers = []
    for part in range(4):
        hops = [(0, every, 1), (0, every, 3), (0, every, 2)]
        refs = [(window(part, k, lines), at.along_a(to)) for k, lines, to in hops]
        gathers.append([remote(src, src, gs.at[part, i], gr.at[part, i], to) for i, (src, to) in enumerate(refs)])
    for part in range(4):
        gathers[part][0].start()
        gathers[part][1].start()
        gathers[part][2].start()

    def gathered(part):
        for copy in gathers[part]:
            copy.wait_recv()

    def held(part, i):
        return slice((3 * part + i) * half, (3 * part + i + 1) * half)

    def product(part, k):
        left = cot_a if part == 0 else normed_a
        cols = pl.ds(pl.multiple_of(((b + k) % 4) * half, half), half)
        return jnp.dot(parts_a[part], left[:, cols], preferred_element_type=F32)

    sums = []
    for part in range(4):
        out = [wo.at[held(part, i), :] for i in range(3)]
        sums.append(
            Ring(
                functools.partial(product, part), out, own_part.at[part], far_in.at[part], near_in.at[part],
                qs.at[part], qr.at[part], at.along_b,
            )
        )

    cot_far, cot_near = spread_ends(cot_full, cot_a, cs, cr, cl)

    def attn_term(shard):
        return jnp.dot(wo[shard_rows(shard), :], parts_a[0, :, mine], preferred_element_type=F32)

    def dn_term(shard):
        rows_of = shard_rows(shard)
        terms = (jnp.dot(wq[t, rows_of, :], parts_a[t + 1, :, mine], preferred_element_type=F32) for t in range(3))
        return sum(terms)

    class ChipSum:
        def __init__(self, term, out, into, send, recv):
            self.term, self.out, self.into = term, out, into
            self.copies = [remote(out.at[k], into.at[k], send.at[k], recv.at[k], at.sibling()) for k in range(4)]

        def start(self):
            for k in (2, 1, 3, 0):
                self.out[k] = self.term(((z + k) % 4) * 2 + 1 - c).astype(BF16)
                self.copies[k].start()

        def sum(self, k):
            value = self.term(((z + k) % 4) * 2 + c)
            self.copies[k].wait()
            return value + self.into[k].astype(F32)

    attn_chip = ChipSum(attn_term, sib_out, sib_in, ss, sr)
    dn_chip = ChipSum(dn_term, dn_sib_out, dn_sib_in, dss, dsr)
    attn_out = [z_out.at[i] for i in range(3)]
    dn_out = [dn_z_out.at[i] for i in range(3)]
    attn_ring = Ring(attn_chip.sum, attn_out, own_at, z_in.at[0], z_in.at[1:3], zs, zr, at.along_z)
    dn_ring = Ring(dn_chip.sum, dn_out, own_dn, dn_z_in.at[0], dn_z_in.at[1:3], dzs, dzr, at.along_z)

    attn_chip.start()
    dn_chip.start()
    attn_ring.send_far()
    dn_ring.send_far()
    attn_ring.send_near()
    dn_ring.send_near()
    cots.finish()
    for copy in cot_far + cot_near:
        copy.wait()
    gathered(0)
    sums[0].send_far()
    norms.finish()
    normed_far, normed_near = spread_ends(normed_full, normed_a, ns, nr, nl)
    for copy in normed_far + normed_near:
        copy.wait()
    for part in (1, 2, 3):
        gathered(part)
        sums[part].send_far()
        sums[part - 1].send_near()
    sums[3].send_near()

    stores = [pltpu.make_async_copy(output, output_to, osem.at[0]), pltpu.make_async_copy(input_grad, input_grad_to, osem.at[1])]
    stores.append(pltpu.make_async_copy(out_grad, out_grad_to, osem.at[2]))
    stores += [pltpu.make_async_copy(qkv_grad.at[t], qkv_grad_to.at[t], osem.at[3 + t]) for t in range(3)]
    output[...] = (packed[...].astype(F32) + attn_ring.total().T).astype(BF16)
    stores[0].start()
    total = dn_ring.total().T
    rstd = columns[:, 1:2]
    unit = (packed[...].astype(F32) - columns[:, 0:1]) * rstd
    u = total * gain_part
    proj[:, 0:width] = u
    ends = exchange(jnp.sum(u, -1, keepdims=True), jnp.sum(u * unit, -1, keepdims=True), en_out, en_in, ens, enr)
    for copy in ends:
        copy.start()
    for copy in ends:
        copy.wait()
    st_pad[0:8, :] = (en_out[...] + sum(en_in[k] for k in range(7))) * (1.0 / 6144.0)
    means = st_pad[...].T
    unit = (packed[...].astype(F32) - columns[:, 0:1]) * rstd
    grad = rstd * (proj[:, 0:width] - means[:, 0:1] - unit * means[:, 1:2])
    input_grad[...] = (cot[...].astype(F32) + grad).astype(BF16)
    stores[1].start()
    for part in range(4):
        result = (sums[part].total() * scale).T.astype(BF16)
        if part == 0:
            out_grad[...] = result
        else:
            qkv_grad[part - 1] = result
        stores[2 + part].start()
    for ring in sums + [attn_ring, dn_ring]:
        ring.finish()
    for part in range(4):
        for copy in gathers[part]:
            copy.wait_send()
    for copy in stores:
        copy.wait()


def hand_over(*refs):
    sources, results, held, came, went = refs[:4], refs[4:8], refs[8:12], refs[12], refs[13]
    ins = [pltpu.make_async_copy(src, buf, came.at[i]) for i, (src, buf) in enumerate(zip(sources, held))]
    outs = [pltpu.make_async_copy(buf, dst, went.at[i]) for i, (buf, dst) in enumerate(zip(held, results))]
    for copy in ins:
        copy.start()
    for before, after in zip(ins, outs):
        before.wait()
        after.start()
    for copy in outs:
        copy.wait()


def shards(patches, dest_group, dest_row, segment, ln_gain, w_qkv, qk_gain, w_out, cotangent):
    anywhere = pl.BlockSpec(memory_space=pl.ANY)
    dma = pltpu.SemaphoreType.DMA
    V = pltpu.VMEM
    scale = 1.0 / math.sqrt(4096)
    out_shape = (
        jax.ShapeDtypeStruct((256, 768), BF16),
        jax.ShapeDtypeStruct((256, 768), BF16),
        jax.ShapeDtypeStruct((3, 384, 384), BF16),
        jax.ShapeDtypeStruct((384, 384), BF16),
    )
    results = pl.pallas_call(
        functools.partial(whole, scale),
        out_shape=out_shape,
        in_specs=[anywhere] * 9,
        out_specs=(anywhere,) * 4,
        scratch_shapes=[
            V((256, 768), BF16), V((1, 256), jnp.int32), V((1, 256), jnp.int32), V((1, 256), jnp.int32),
            V((1, 6144), F32), V((2, 128), F32), V((256, 768), BF16),
            *(V(shape.shape, BF16) for shape in out_shape),
            V((512, 896), BF16), V((512, 896), BF16), V((256, 768), BF16),
            V((8, 256, 768), BF16), V((8, 256, 768), BF16),
            V((1024, 1536), BF16), V((1024, 1536), BF16), V((4, 384, 1024), BF16),
            V((3, 6144, 384), BF16), V((6144, 384), BF16),
            V((256, 1152), F32), V((256, 384), F32), V((256, 384), BF16), V((256, 1152), BF16),
            V((256, 128), F32), V((256, 128), F32), V((128, 256), F32),
            V((8, 256), F32), V((7, 8, 256), F32), V((8, 256), F32), V((7, 8, 256), F32),
            V((4, 768, 256), BF16), V((4, 768, 256), BF16), V((3, 768, 256), BF16), V((3, 768, 256), BF16),
            V((4, 768, 256), BF16), V((4, 768, 256), BF16), V((3, 768, 256), BF16), V((3, 768, 256), BF16),
            V((4, 384, 384), BF16), V((4, 2, 384, 384), BF16),
            V((4, 384, 384), F32), V((768, 256), F32), V((768, 256), F32),
            dma((8,)), dma((6,)), dma((2,)), dma((15,)), dma((15,)),
            dma((2, 4)), dma((2, 4)), dma((2, 4)), dma((2, 4)), dma((2, 4)), dma((2, 4)), dma((2, 4)), dma((2, 4)),
            dma((7,)), dma((7,)), dma((7,)), dma((7,)),
            dma((2, 3, 4)), dma((2, 3, 4)), dma((2, 4)), dma((2, 3, 4)), dma((2, 3, 4)), dma((2, 4)),
            dma((4, 4)), dma((4, 4)),
            dma((4,)), dma((4,)), dma((4,)), dma((4,)), dma((4,)), dma((4,)), dma((4,)), dma((4,)),
            dma((4, 4)), dma((4, 4)),
        ],
        compiler_params=pltpu.CompilerParams(
            collective_id=1, has_side_effects=True, vmem_limit_bytes=62 << 20
        ),
        name="whole",
    )(
        patches, dest_group.reshape(1, 256), dest_row.reshape(1, 256), segment.reshape(1, 256),
        ln_gain.reshape(1, 6144), jnp.transpose(w_qkv, (1, 0, 2)), qk_gain, w_out, cotangent,
    )
    output, input_grad, qkv_grad, out_grad = pl.pallas_call(
        hand_over,
        out_shape=out_shape,
        in_specs=[anywhere] * 4,
        out_specs=(anywhere,) * 4,
        scratch_shapes=[V(shape.shape, BF16) for shape in out_shape] + [dma((4,)), dma((4,))],
        name="hand_over",
    )(*results)
    return (output, input_grad, jnp.transpose(qkv_grad, (1, 0, 2)), out_grad)


def solution(mesh):
    placed = (
        P("dp", "mp"),
        P("dp"),
        P("dp"),
        P("dp"),
        P(),
        P(None, None, "mp"),
        P(),
        P(None, "mp"),
        P("dp", "mp"),
    )
    return jax.shard_map(
        shards,
        mesh=mesh,
        in_specs=placed,
        out_specs=(P("dp", "mp"), P("dp", "mp"), P("dp", None, "mp"), P("dp", "mp")),
        check_vma=False,
    )
```

```python
import functools
import math

import jax
import jax.numpy as jnp
from jax import lax
from jax.experimental import pallas as pl
from jax.experimental.pallas import tpu as pltpu
from jax.sharding import PartitionSpec as P

DH = 128
MESH = pl.DeviceIdType.MESH
F32 = jnp.float32
BF16 = jnp.bfloat16


class Place:
    def __init__(self):
        self.g, self.m = lax.axis_index("dp"), lax.axis_index("mp")
        self.x, self.y = self.g // 4, self.g % 4
        self.z, self.c = self.m // 2, self.m % 2
        c = self.c
        self.a = self.x * (1 - c) + self.y * c
        self.b = self.x * c + self.y * (1 - c)

    def along_a(self, k):
        x, y = (self.x + k * (1 - self.c)) % 4, (self.y + k * self.c) % 4
        return (x * 4 + y, self.m)

    def along_b(self, k):
        x, y = (self.x + k * self.c) % 4, (self.y + k * (1 - self.c)) % 4
        return (x * 4 + y, self.m)

    def along_z(self, k):
        return (self.g, ((self.z + k) % 4) * 2 + self.c)

    def along_m(self, k):
        return (self.g, (self.m + k) % 8)

    def over_xy(self, dx, dy):
        return (((self.x + dx) % 4) * 4 + (self.y + dy) % 4, self.m)

    def sibling(self):
        return (self.g, self.z * 2 + 1 - self.c)

    def block(self, q, j):
        c = self.c
        return 4 * (q * (1 - c) + j * c) + q * c + j * (1 - c)


def remote(src, dst, send, recv, device):
    return pltpu.make_async_remote_copy(
        src_ref=src, dst_ref=dst, send_sem=send, recv_sem=recv, device_id=device, device_id_type=MESH
    )


def nt_dot(left, right):
    return lax.dot_general(left, right, (((1,), (1,)), ((), ())), preferred_element_type=F32)


def tn_dot(left, right):
    return lax.dot_general(left, right, (((0,), (0,)), ((), ())), preferred_element_type=F32)


class Ring:
    def __init__(self, term, out, own, far_in, near_in, send, recv, along):
        size = own.shape[0]
        self.low, self.high = slice(0, size // 2), slice(size // 2, size)
        self.term, self.out, self.own, self.far_in, self.near_in = term, out, own, far_in, near_in
        pairs = [
            (out[0].at[self.low, :], far_in.at[self.low, :], 1),
            (out[0].at[self.high, :], far_in.at[self.high, :], 3),
            (out[1], near_in.at[0], 1),
            (out[2], near_in.at[1], 3),
        ]
        self.copies = [remote(src, dst, send.at[i], recv.at[i], along(to)) for i, (src, dst, to) in enumerate(pairs)]

    def send_far(self):
        self.out[0][...] = self.term(2).astype(BF16)
        self.copies[0].start()
        self.copies[1].start()

    def send_near(self):
        for i, k in enumerate((1, 3)):
            self.own[...] = self.term(k)
            self.copies[i].wait_recv()
            lines = (self.low, self.high)[i]
            self.own[lines, :] += self.far_in[lines, :].astype(F32)
            self.out[1 + i][...] = self.own[...].astype(BF16)
            self.copies[2 + i].start()
        self.own[...] = self.term(0)

    def total(self):
        self.copies[2].wait_recv()
        self.copies[3].wait_recv()
        return self.own[...] + self.near_in[0].astype(F32) + self.near_in[1].astype(F32)

    def finish(self):
        for copy in self.copies:
            copy.wait_send()


def whole(
    scale,
    patches_in, dest_group_in, dest_row_in, segment_in, gain_in, w_qkv, qk_gain_in, w_out, cot_in,
    output_to, input_grad_to, qkv_grad_to, out_grad_to,
    patches, dest_group, dest_row, segment, gain, qk_gain, cot, output, input_grad, qkv_grad, out_grad,
    outbox, inbox, packed, cot_full, normed_full, cot_a, normed_a, parts_a, wq, wo,
    proj, d_heads, heads, dproj, columns, places, st_pad, st_out, st_in, en_out, en_in,
    sib_out, sib_in, z_out, z_in, dn_sib_out, dn_sib_in, dn_z_out, dn_z_in, far_in, near_in,
    own_part, own_at, own_dn,
    isem, osem, wsem, rs, rr, cz, czr, cb, cbr, nz, nzr, nb, nbr, sts, str_, ens, enr,
    cs, cr, cl, ns, nr, nl, gs, gr, ss, sr, zs, zr, dss, dsr, dzs, dzr, qs, qr,
):
    at = Place()
    a, b, c, z, m, g = at.a, at.b, at.c, at.z, at.m, at.g
    width, half, rows = 768, 384, 256
    load_wo = pltpu.make_async_copy(w_out, wo, wsem.at[0])
    load_wq = pltpu.make_async_copy(w_qkv, wq, wsem.at[1])
    pairs = [
        (dest_group_in, dest_group), (dest_row_in, dest_row), (segment_in, segment), (patches_in, patches),
        (cot_in, cot_full.at[m]), (cot_in, cot), (gain_in, gain), (qk_gain_in, qk_gain),
    ]
    loads = [pltpu.make_async_copy(src, dst, isem.at[i]) for i, (src, dst) in enumerate(pairs)]
    over_dp = [(dx, dy) for dx in range(4) for dy in range(4) if dx + dy > 0]
    barrier = pltpu.get_barrier_semaphore()
    met = [at.over_xy(dx, dy) for dx, dy in over_dp] + [at.along_m(k) for k in range(1, 8)]
    for device in met:
        pl.semaphore_signal(barrier, inc=1, device_id=device, device_id_type=MESH)
    for copy in loads + [load_wo, load_wq]:
        copy.start()
    for copy in loads[0:4]:
        copy.wait()

    group_row = dest_group[...]
    member = (lax.broadcasted_iota(jnp.int32, (16, rows), 0) == group_row).astype(F32)
    before = (
        lax.broadcasted_iota(jnp.int32, (rows, rows), 0) < lax.broadcasted_iota(jnp.int32, (rows, rows), 1)
    ).astype(BF16)
    rank = jnp.sum(jnp.dot(member.astype(BF16), before, preferred_element_type=F32) * member, 0, keepdims=True)
    slot = group_row.astype(F32) * 32.0 + rank
    pick = (lax.broadcasted_iota(jnp.int32, (512, rows), 0).astype(F32) == slot).astype(BF16)
    st_pad[...] = jnp.zeros_like(st_pad)
    st_pad[0:1, :] = dest_row[...].astype(F32) + 1.0
    st_pad[1:2, :] = segment[...].astype(F32)
    places[...] = st_pad[...].T
    address = jnp.broadcast_to(places[:, 0:1], (rows, 128)).astype(BF16)
    outbox[:, 0:width] = jnp.dot(pick, patches[...], preferred_element_type=F32).astype(BF16)
    outbox[:, width:] = jnp.dot(pick, address, preferred_element_type=F32).astype(BF16)
    for copy in loads[4:]:
        copy.wait()
    pl.semaphore_wait(barrier, len(met))

    here = pl.ds(pl.multiple_of(g * 32, 32), 32)
    routes = []
    for i, (dx, dy) in enumerate(over_dp):
        device = at.over_xy(dx, dy)
        there = pl.ds(pl.multiple_of(device[0] * 32, 32), 32)
        routes.append(remote(outbox.at[there, :], inbox.at[here, :], rs.at[i], rr.at[i], device))
    for copy in routes:
        copy.start()
    inbox[here, :] = outbox[here, :]

    class Collect:
        def __init__(self, full, z_send, z_recv, b_send, b_recv):
            up, down = at.along_z(1), at.along_z(3)
            self.z, self.b = [], []
            for h in (0, 1):
                part, low, high = (slice(128 * h + i, 128 * h + j) for i, j in ((0, 128), (0, 64), (64, 128)))
                own = full.at[m, part, :]
                hops = [(own, up), (own, down), (full.at[self.mine(1), low, :], up), (full.at[self.mine(3), high, :], down)]
                self.z.append([remote(src, src, z_send.at[h, i], z_recv.at[h, i], to) for i, (src, to) in enumerate(hops)])
                slabs = [full.at[self.mine(k), part, :] for k in range(4)]
                self.b.append([remote(slabs[k], slabs[k], b_send.at[h, k], b_recv.at[h, k], at.sibling()) for k in range(4)])

        def mine(self, k):
            return ((z + 4 - k) % 4) * 2 + c

        def others(self, k):
            return ((z + 4 - k) % 4) * 2 + 1 - c

        def start(self):
            for h in (0, 1):
                self.z[h][0].start()
                self.z[h][1].start()
                self.b[h][0].start()

        def near(self, h):
            for i in (0, 1):
                self.z[h][i].wait_recv()
                self.z[h][2 + i].start()
                self.b[h][1 + 2 * i].start()

        def far(self, h):
            self.z[h][2].wait_recv()
            self.z[h][3].wait_recv()
            self.b[h][2].start()

        def other(self, k, h):
            self.b[h][k].wait_recv()

        def finish(self):
            for copy in self.z[0] + self.z[1] + self.b[0] + self.b[1]:
                copy.wait_send()

    mine = pl.ds(pl.multiple_of(a * rows, rows), rows)

    def spread_slab(full, s, half_of, buf, send, recv, near):
        lines = pl.ds(pl.multiple_of(a * rows + 128 * half_of, 128), 128)
        for h in (0, 1):
            bx, by = (2 * s + h) // 4, (2 * s + h) % 4
            q, j = bx * (1 - c) + by * c, bx * c + by * (1 - c)
            k = (q - a + 4) % 4
            n = (k + 3) % 4
            src = full.at[s, 128 * half_of : 128 * half_of + 128, pl.ds(h * half, half)]
            dst = buf.at[lines, pl.ds(pl.multiple_of(j * half, half), half)]

            @pl.when(k == 0)
            def _():
                pltpu.make_async_copy(src, dst, near.at[half_of, j]).start()

            @pl.when(k != 0)
            def _():
                remote(src, dst, send.at[half_of, n, j], recv.at[half_of, n, j], at.along_a(k)).start()

    def spread_ends(full, buf, send, recv, near):
        src, dst = full.at[0, 0:128, 0:half], buf.at[0:128, 0:half]
        far = [
            remote(src, dst, send.at[h, k - 1, j], recv.at[h, k - 1, j], at.along_a(k))
            for h in (0, 1)
            for k in (1, 2, 3)
            for j in range(4)
        ]
        local = [pltpu.make_async_copy(src, dst, near.at[h, j]) for h in (0, 1) for j in range(4)]
        return far, local

    def shard_rows(s):
        return pl.ds(pl.multiple_of(s * width, width), width)

    cots = Collect(cot_full, cz, czr, cb, cbr)
    cots.start()
    load_wo.wait()

    def add_heads(s, first=False):
        term = jnp.dot(cot_full[s], wo[shard_rows(s), :], preferred_element_type=F32)
        d_heads[...] = term if first else d_heads[...] + term

    def spread_cot(s, h):
        spread_slab(cot_full, s, h, cot_a, cs, cr, cl)

    add_heads(m, True)
    cots.near(0)
    cots.other(0, 0)
    cots.other(0, 1)
    add_heads(cots.others(0))
    cots.near(1)
    cots.far(0)
    add_heads(cots.mine(1))
    add_heads(cots.mine(3))

    for copy in routes:
        copy.wait()
    arrived = inbox[:, width : width + 1].astype(F32)
    put = (lax.broadcasted_iota(jnp.int32, (512, rows), 1).astype(F32) + 1.0 == arrived).astype(BF16)
    block = tn_dot(put, inbox[:, 0:width])
    packed[...] = block.astype(BF16)

    def exchange(first, second, out, into, send, recv):
        lane = lax.broadcasted_iota(jnp.int32, (rows, 128), 1)
        out[...] = jnp.where(lane == 0, first, jnp.where(lane == 1, second, 0.0)).T[0:8]
        return [remote(out, into.at[k - 1], send.at[k - 1], recv.at[k - 1], at.along_m(k)) for k in range(1, 8)]

    part_mean = jnp.mean(block, -1, keepdims=True)
    part_center = block - part_mean
    stats = exchange(part_mean, jnp.sum(part_center * part_center, -1, keepdims=True), st_out, st_in, sts, str_)
    for copy in stats:
        copy.start()

    for h in (0, 1):
        spread_cot(m, h)
        spread_cot(cots.others(0), h)
        for k in (1, 3):
            spread_cot(cots.mine(k), h)
            cots.other(k, h)
            spread_cot(cots.others(k), h)
    spread_cot(cots.mine(2), 0)
    for copy in stats:
        copy.wait()
    parts = [st_out[...]] + [st_in[k] for k in range(7)]
    mean = sum(part[0:1] for part in parts) * 0.125
    spread = sum(part[1:2] + width * (part[0:1] - mean) * (part[0:1] - mean) for part in parts)
    st_pad[0:1, :] = mean
    st_pad[1:2, :] = lax.rsqrt(spread * (1.0 / 6144.0) + 1e-06)
    columns[...] = st_pad[...].T
    gain_part = gain[:, pl.ds(pl.multiple_of(m * width, width), width)]
    unit = (packed[...].astype(F32) - columns[:, 0:1]) * columns[:, 1:2]
    normed_full[m] = (unit * gain_part).astype(BF16)
    norms = Collect(normed_full, nz, nzr, nb, nbr)
    norms.start()

    def spread_normed(s, h):
        spread_slab(normed_full, s, h, normed_a, ns, nr, nl)

    def add_projected(s, first=False):
        for t in range(3):
            cols = slice(t * half, (t + 1) * half)
            term = jnp.dot(normed_full[s], wq[t, shard_rows(s), :], preferred_element_type=F32)
            proj[:, cols] = term if first else proj[:, cols] + term

    cots.far(1)
    spread_cot(cots.mine(2), 1)
    for h in (0, 1):
        cots.other(2, h)
        spread_cot(cots.others(2), h)
    for h in (0, 1):
        spread_normed(m, h)
    norms.near(0)
    for k in (1, 3):
        spread_normed(norms.mine(k), 0)
    for h in (0, 1):
        norms.other(0, h)
        spread_normed(norms.others(0), h)
    load_wq.wait()
    add_projected(m, True)
    add_projected(norms.others(0))
    for k in (1, 3):
        norms.other(k, 0)
        spread_normed(norms.others(k), 0)
    for s in (cots.others(1), cots.others(3), cots.mine(2), cots.others(2)):
        add_heads(s)
    norms.near(1)
    norms.far(0)
    spread_normed(norms.mine(2), 0)
    for k in (1, 3):
        spread_normed(norms.mine(k), 1)
        add_projected(norms.mine(k))
    norms.other(2, 0)
    spread_normed(norms.others(2), 0)
    for k in (1, 3):
        norms.other(k, 1)
        spread_normed(norms.others(k), 1)
    for k in (1, 3):
        add_projected(norms.others(k))
    norms.far(1)
    spread_normed(norms.mine(2), 1)
    norms.other(2, 1)
    spread_normed(norms.others(2), 1)
    add_projected(norms.mine(2))
    add_projected(norms.others(2))
    same = places[:, 1:2] == segment[...].astype(F32)

    def normalise(values):
        center = values - jnp.mean(values, -1, keepdims=True)
        inverse = lax.rsqrt(jnp.mean(center * center, -1, keepdims=True) + 1e-06)
        return center * inverse, inverse

    def normalise_back(grad, unit, inverse, weight):
        scaled = grad.astype(BF16).astype(F32) * weight
        inner = scaled - jnp.mean(scaled, -1, keepdims=True) - unit * jnp.mean(scaled * unit, -1, keepdims=True)
        return (inverse * inner).astype(BF16)

    root = DH ** (-0.5)
    for h in range(3):
        q_cols, k_cols, v_cols = (slice(t * half + h * DH, t * half + (h + 1) * DH) for t in range(3))
        h_cols = slice(h * DH, (h + 1) * DH)
        unit_q, inverse_q = normalise(proj[:, q_cols])
        unit_k, inverse_k = normalise(proj[:, k_cols])
        queries = (unit_q * qk_gain[0:1, :]).astype(BF16)
        keys = (unit_k * qk_gain[1:2, :]).astype(BF16)
        values = proj[:, v_cols].astype(BF16)
        raised = jnp.where(same, jnp.exp(nt_dot(queries, keys) * root), 0.0)
        exact = raised / jnp.sum(raised, -1, keepdims=True)
        weights = exact.astype(BF16)
        heads[:, h_cols] = jnp.dot(weights, values, preferred_element_type=F32).astype(BF16)
        given = d_heads[:, h_cols].astype(BF16)
        d_weights = nt_dot(given, values).astype(BF16).astype(F32)
        dproj[:, v_cols] = tn_dot(weights, given).astype(BF16)
        inner = jnp.sum(d_weights * exact, -1, keepdims=True)
        d_scores = (exact * (d_weights - inner) * root).astype(BF16)
        d_queries = jnp.dot(d_scores, keys, preferred_element_type=F32)
        d_keys = tn_dot(d_scores, queries)
        dproj[:, q_cols] = normalise_back(d_queries, unit_q, inverse_q, qk_gain[0:1, :])
        dproj[:, k_cols] = normalise_back(d_keys, unit_k, inverse_k, qk_gain[1:2, :])

    for part in range(4):
        block = heads[...] if part == 0 else dproj[:, (part - 1) * half : part * half]
        parts_a[part, :, mine] = block.T

    def window(part, k, lines):
        cols = pl.ds(pl.multiple_of(((a + k) % 4) * rows, rows), rows)
        return parts_a.at[part, lines, cols]

    low, high, every = slice(0, 192), slice(192, 384), slice(0, 384)
    gathers = []
    for part in range(4):
        hops = [(0, every, 1), (0, every, 3), (0, every, 2)]
        refs = [(window(part, k, lines), at.along_a(to)) for k, lines, to in hops]
        gathers.append([remote(src, src, gs.at[part, i], gr.at[part, i], to) for i, (src, to) in enumerate(refs)])
    for part in range(4):
        gathers[part][0].start()
        gathers[part][1].start()
        gathers[part][2].start()

    def gathered(part):
        for copy in gathers[part]:
            copy.wait_recv()

    def held(part, i):
        return slice((3 * part + i) * half, (3 * part + i + 1) * half)

    def product(part, k):
        left = cot_a if part == 0 else normed_a
        cols = pl.ds(pl.multiple_of(((b + k) % 4) * half, half), half)
        return jnp.dot(parts_a[part], left[:, cols], preferred_element_type=F32)

    sums = []
    for part in range(4):
        out = [wo.at[held(part, i), :] for i in range(3)]
        sums.append(
            Ring(
                functools.partial(product, part), out, own_part.at[part], far_in.at[part], near_in.at[part],
                qs.at[part], qr.at[part], at.along_b,
            )
        )

    cot_far, cot_near = spread_ends(cot_full, cot_a, cs, cr, cl)

    def attn_term(shard):
        return jnp.dot(wo[shard_rows(shard), :], parts_a[0, :, mine], preferred_element_type=F32)

    def dn_term(shard):
        rows_of = shard_rows(shard)
        terms = (jnp.dot(wq[t, rows_of, :], parts_a[t + 1, :, mine], preferred_element_type=F32) for t in range(3))
        return sum(terms)

    class ChipSum:
        def __init__(self, term, out, into, send, recv):
            self.term, self.out, self.into = term, out, into
            self.copies = [remote(out.at[k], into.at[k], send.at[k], recv.at[k], at.sibling()) for k in range(4)]

        def start(self):
            for k in (2, 1, 3, 0):
                self.out[k] = self.term(((z + k) % 4) * 2 + 1 - c).astype(BF16)
                self.copies[k].start()

        def sum(self, k):
            value = self.term(((z + k) % 4) * 2 + c)
            self.copies[k].wait()
            return value + self.into[k].astype(F32)

    attn_chip = ChipSum(attn_term, sib_out, sib_in, ss, sr)
    dn_chip = ChipSum(dn_term, dn_sib_out, dn_sib_in, dss, dsr)
    attn_out = [z_out.at[i] for i in range(3)]
    dn_out = [dn_z_out.at[i] for i in range(3)]
    attn_ring = Ring(attn_chip.sum, attn_out, own_at, z_in.at[0], z_in.at[1:3], zs, zr, at.along_z)
    dn_ring = Ring(dn_chip.sum, dn_out, own_dn, dn_z_in.at[0], dn_z_in.at[1:3], dzs, dzr, at.along_z)

    attn_chip.start()
    dn_chip.start()
    attn_ring.send_far()
    dn_ring.send_far()
    attn_ring.send_near()
    dn_ring.send_near()
    cots.finish()
    for copy in cot_far + cot_near:
        copy.wait()
    gathered(0)
    sums[0].send_far()
    norms.finish()
    normed_far, normed_near = spread_ends(normed_full, normed_a, ns, nr, nl)
    for copy in normed_far + normed_near:
        copy.wait()
    sums[0].send_near()
    for part in (1, 2, 3):
        gathered(part)
        sums[part].send_far()
    sums[1].send_near()
    sums[2].send_near()
    sums[3].send_near()

    stores = [pltpu.make_async_copy(output, output_to, osem.at[0]), pltpu.make_async_copy(input_grad, input_grad_to, osem.at[1])]
    stores.append(pltpu.make_async_copy(out_grad, out_grad_to, osem.at[2]))
    stores += [pltpu.make_async_copy(qkv_grad.at[t], qkv_grad_to.at[t], osem.at[3 + t]) for t in range(3)]
    output[...] = (packed[...].astype(F32) + attn_ring.total().T).astype(BF16)
    stores[0].start()
    total = dn_ring.total().T
    rstd = columns[:, 1:2]
    unit = (packed[...].astype(F32) - columns[:, 0:1]) * rstd
    u = total * gain_part
    proj[:, 0:width] = u
    ends = exchange(jnp.sum(u, -1, keepdims=True), jnp.sum(u * unit, -1, keepdims=True), en_out, en_in, ens, enr)
    for copy in ends:
        copy.start()
    for copy in ends:
        copy.wait()
    st_pad[0:8, :] = (en_out[...] + sum(en_in[k] for k in range(7))) * (1.0 / 6144.0)
    means = st_pad[...].T
    unit = (packed[...].astype(F32) - columns[:, 0:1]) * rstd
    grad = rstd * (proj[:, 0:width] - means[:, 0:1] - unit * means[:, 1:2])
    input_grad[...] = (cot[...].astype(F32) + grad).astype(BF16)
    stores[1].start()
    for part in range(4):
        result = (sums[part].total() * scale).T.astype(BF16)
        if part == 0:
            out_grad[...] = result
        else:
            qkv_grad[part - 1] = result
        stores[2 + part].start()
    for ring in sums + [attn_ring, dn_ring]:
        ring.finish()
    for part in range(4):
        for copy in gathers[part]:
            copy.wait_send()
    for copy in stores:
        copy.wait()


def hand_over(*refs):
    sources, results, held, came, went = refs[:4], refs[4:8], refs[8:12], refs[12], refs[13]
    ins = [pltpu.make_async_copy(src, buf, came.at[i]) for i, (src, buf) in enumerate(zip(sources, held))]
    outs = [pltpu.make_async_copy(buf, dst, went.at[i]) for i, (buf, dst) in enumerate(zip(held, results))]
    for copy in ins:
        copy.start()
    for before, after in zip(ins, outs):
        before.wait()
        after.start()
    for copy in outs:
        copy.wait()


def shards(patches, dest_group, dest_row, segment, ln_gain, w_qkv, qk_gain, w_out, cotangent):
    anywhere = pl.BlockSpec(memory_space=pl.ANY)
    dma = pltpu.SemaphoreType.DMA
    V = pltpu.VMEM
    scale = 1.0 / math.sqrt(4096)
    out_shape = (
        jax.ShapeDtypeStruct((256, 768), BF16),
        jax.ShapeDtypeStruct((256, 768), BF16),
        jax.ShapeDtypeStruct((3, 384, 384), BF16),
        jax.ShapeDtypeStruct((384, 384), BF16),
    )
    results = pl.pallas_call(
        functools.partial(whole, scale),
        out_shape=out_shape,
        in_specs=[anywhere] * 9,
        out_specs=(anywhere,) * 4,
        scratch_shapes=[
            V((256, 768), BF16), V((1, 256), jnp.int32), V((1, 256), jnp.int32), V((1, 256), jnp.int32),
            V((1, 6144), F32), V((2, 128), F32), V((256, 768), BF16),
            *(V(shape.shape, BF16) for shape in out_shape),
            V((512, 896), BF16), V((512, 896), BF16), V((256, 768), BF16),
            V((8, 256, 768), BF16), V((8, 256, 768), BF16),
            V((1024, 1536), BF16), V((1024, 1536), BF16), V((4, 384, 1024), BF16),
            V((3, 6144, 384), BF16), V((6144, 384), BF16),
            V((256, 1152), F32), V((256, 384), F32), V((256, 384), BF16), V((256, 1152), BF16),
            V((256, 128), F32), V((256, 128), F32), V((128, 256), F32),
            V((8, 256), F32), V((7, 8, 256), F32), V((8, 256), F32), V((7, 8, 256), F32),
            V((4, 768, 256), BF16), V((4, 768, 256), BF16), V((3, 768, 256), BF16), V((3, 768, 256), BF16),
            V((4, 768, 256), BF16), V((4, 768, 256), BF16), V((3, 768, 256), BF16), V((3, 768, 256), BF16),
            V((4, 384, 384), BF16), V((4, 2, 384, 384), BF16),
            V((4, 384, 384), F32), V((768, 256), F32), V((768, 256), F32),
            dma((8,)), dma((6,)), dma((2,)), dma((15,)), dma((15,)),
            dma((2, 4)), dma((2, 4)), dma((2, 4)), dma((2, 4)), dma((2, 4)), dma((2, 4)), dma((2, 4)), dma((2, 4)),
            dma((7,)), dma((7,)), dma((7,)), dma((7,)),
            dma((2, 3, 4)), dma((2, 3, 4)), dma((2, 4)), dma((2, 3, 4)), dma((2, 3, 4)), dma((2, 4)),
            dma((4, 4)), dma((4, 4)),
            dma((4,)), dma((4,)), dma((4,)), dma((4,)), dma((4,)), dma((4,)), dma((4,)), dma((4,)),
            dma((4, 4)), dma((4, 4)),
        ],
        compiler_params=pltpu.CompilerParams(
            collective_id=1, has_side_effects=True, vmem_limit_bytes=62 << 20
        ),
        name="whole",
    )(
        patches, dest_group.reshape(1, 256), dest_row.reshape(1, 256), segment.reshape(1, 256),
        ln_gain.reshape(1, 6144), jnp.transpose(w_qkv, (1, 0, 2)), qk_gain, w_out, cotangent,
    )
    output, input_grad, qkv_grad, out_grad = pl.pallas_call(
        hand_over,
        out_shape=out_shape,
        in_specs=[anywhere] * 4,
        out_specs=(anywhere,) * 4,
        scratch_shapes=[V(shape.shape, BF16) for shape in out_shape] + [dma((4,)), dma((4,))],
        name="hand_over",
    )(*results)
    return (output, input_grad, jnp.transpose(qkv_grad, (1, 0, 2)), out_grad)


def solution(mesh):
    placed = (
        P("dp", "mp"),
        P("dp"),
        P("dp"),
        P("dp"),
        P(),
        P(None, None, "mp"),
        P(),
        P(None, "mp"),
        P("dp", "mp"),
    )
    return jax.shard_map(
        shards,
        mesh=mesh,
        in_specs=placed,
        out_specs=(P("dp", "mp"), P("dp", "mp"), P("dp", None, "mp"), P("dp", "mp")),
        check_vma=False,
    )
```

```python
import functools
import math

import jax
import jax.numpy as jnp
from jax import lax
from jax.experimental import pallas as pl
from jax.experimental.pallas import tpu as pltpu
from jax.sharding import PartitionSpec as P

DH = 128
MESH = pl.DeviceIdType.MESH
F32 = jnp.float32
BF16 = jnp.bfloat16


class Place:
    def __init__(self):
        self.g, self.m = lax.axis_index("dp"), lax.axis_index("mp")
        self.x, self.y = self.g // 4, self.g % 4
        self.z, self.c = self.m // 2, self.m % 2
        c = self.c
        self.a = self.x * (1 - c) + self.y * c
        self.b = self.x * c + self.y * (1 - c)

    def along_a(self, k):
        x, y = (self.x + k * (1 - self.c)) % 4, (self.y + k * self.c) % 4
        return (x * 4 + y, self.m)

    def along_b(self, k):
        x, y = (self.x + k * self.c) % 4, (self.y + k * (1 - self.c)) % 4
        return (x * 4 + y, self.m)

    def along_z(self, k):
        return (self.g, ((self.z + k) % 4) * 2 + self.c)

    def along_m(self, k):
        return (self.g, (self.m + k) % 8)

    def over_xy(self, dx, dy):
        return (((self.x + dx) % 4) * 4 + (self.y + dy) % 4, self.m)

    def sibling(self):
        return (self.g, self.z * 2 + 1 - self.c)

    def block(self, q, j):
        c = self.c
        return 4 * (q * (1 - c) + j * c) + q * c + j * (1 - c)


def remote(src, dst, send, recv, device):
    return pltpu.make_async_remote_copy(
        src_ref=src, dst_ref=dst, send_sem=send, recv_sem=recv, device_id=device, device_id_type=MESH
    )


def nt_dot(left, right):
    return lax.dot_general(left, right, (((1,), (1,)), ((), ())), preferred_element_type=F32)


def tn_dot(left, right):
    return lax.dot_general(left, right, (((0,), (0,)), ((), ())), preferred_element_type=F32)


class Ring:
    def __init__(self, term, out, own, far_in, near_in, send, recv, along):
        size = own.shape[0]
        self.low, self.high = slice(0, size // 2), slice(size // 2, size)
        self.term, self.out, self.own, self.far_in, self.near_in = term, out, own, far_in, near_in
        pairs = [
            (out[0].at[self.low, :], far_in.at[self.low, :], 1),
            (out[0].at[self.high, :], far_in.at[self.high, :], 3),
            (out[1], near_in.at[0], 1),
            (out[2], near_in.at[1], 3),
        ]
        self.copies = [remote(src, dst, send.at[i], recv.at[i], along(to)) for i, (src, dst, to) in enumerate(pairs)]

    def send_far(self):
        self.out[0][...] = self.term(2).astype(BF16)
        self.copies[0].start()
        self.copies[1].start()

    def send_near(self):
        for i, k in enumerate((1, 3)):
            self.own[...] = self.term(k)
            self.copies[i].wait_recv()
            lines = (self.low, self.high)[i]
            self.own[lines, :] += self.far_in[lines, :].astype(F32)
            self.out[1 + i][...] = self.own[...].astype(BF16)
            self.copies[2 + i].start()
        self.own[...] = self.term(0)

    def total(self):
        self.copies[2].wait_recv()
        self.copies[3].wait_recv()
        return self.own[...] + self.near_in[0].astype(F32) + self.near_in[1].astype(F32)

    def finish(self):
        for copy in self.copies:
            copy.wait_send()


def whole(
    scale,
    patches_in, dest_group_in, dest_row_in, segment_in, gain_in, w_qkv, qk_gain_in, w_out, cot_in,
    output_to, input_grad_to, qkv_grad_to, out_grad_to,
    patches, dest_group, dest_row, segment, gain, qk_gain, cot, output, input_grad, qkv_grad, out_grad,
    outbox, inbox, packed, cot_full, normed_full, cot_a, normed_a, parts_a, wq, wo,
    proj, d_heads, heads, dproj, columns, places, st_pad, st_out, st_in, en_out, en_in,
    sib_out, sib_in, z_out, z_in, dn_sib_out, dn_sib_in, dn_z_out, dn_z_in, far_in, near_in,
    own_part, own_at, own_dn,
    isem, osem, wsem, rs, rr, cz, czr, cb, cbr, nz, nzr, nb, nbr, sts, str_, ens, enr,
    cs, cr, cl, ns, nr, nl, gs, gr, ss, sr, zs, zr, dss, dsr, dzs, dzr, qs, qr,
):
    at = Place()
    a, b, c, z, m, g = at.a, at.b, at.c, at.z, at.m, at.g
    width, half, rows = 768, 384, 256
    load_wo = pltpu.make_async_copy(w_out, wo, wsem.at[0])
    load_wq = pltpu.make_async_copy(w_qkv, wq, wsem.at[1])
    pairs = [
        (dest_group_in, dest_group), (dest_row_in, dest_row), (segment_in, segment), (patches_in, patches),
        (cot_in, cot_full.at[m]), (cot_in, cot), (gain_in, gain), (qk_gain_in, qk_gain),
    ]
    loads = [pltpu.make_async_copy(src, dst, isem.at[i]) for i, (src, dst) in enumerate(pairs)]
    over_dp = [(dx, dy) for dx in range(4) for dy in range(4) if dx + dy > 0]
    barrier = pltpu.get_barrier_semaphore()
    met = [at.over_xy(dx, dy) for dx, dy in over_dp] + [at.along_m(k) for k in range(1, 8)]
    for device in met:
        pl.semaphore_signal(barrier, inc=1, device_id=device, device_id_type=MESH)
    for copy in loads + [load_wo, load_wq]:
        copy.start()
    for copy in loads[0:4]:
        copy.wait()

    group_row = dest_group[...]
    member = (lax.broadcasted_iota(jnp.int32, (16, rows), 0) == group_row).astype(F32)
    before = (
        lax.broadcasted_iota(jnp.int32, (rows, rows), 0) < lax.broadcasted_iota(jnp.int32, (rows, rows), 1)
    ).astype(BF16)
    rank = jnp.sum(jnp.dot(member.astype(BF16), before, preferred_element_type=F32) * member, 0, keepdims=True)
    slot = group_row.astype(F32) * 32.0 + rank
    pick = (lax.broadcasted_iota(jnp.int32, (512, rows), 0).astype(F32) == slot).astype(BF16)
    st_pad[...] = jnp.zeros_like(st_pad)
    st_pad[0:1, :] = dest_row[...].astype(F32) + 1.0
    st_pad[1:2, :] = segment[...].astype(F32)
    places[...] = st_pad[...].T
    address = jnp.broadcast_to(places[:, 0:1], (rows, 128)).astype(BF16)
    outbox[:, 0:width] = jnp.dot(pick, patches[...], preferred_element_type=F32).astype(BF16)
    outbox[:, width:] = jnp.dot(pick, address, preferred_element_type=F32).astype(BF16)
    for copy in loads[4:]:
        copy.wait()
    pl.semaphore_wait(barrier, len(met))

    here = pl.ds(pl.multiple_of(g * 32, 32), 32)
    routes = []
    for i, (dx, dy) in enumerate(over_dp):
        device = at.over_xy(dx, dy)
        there = pl.ds(pl.multiple_of(device[0] * 32, 32), 32)
        routes.append(remote(outbox.at[there, :], inbox.at[here, :], rs.at[i], rr.at[i], device))
    for copy in routes:
        copy.start()
    inbox[here, :] = outbox[here, :]

    class Collect:
        def __init__(self, full, z_send, z_recv, b_send, b_recv):
            up, down = at.along_z(1), at.along_z(3)
            self.z, self.b = [], []
            for h in (0, 1):
                part, low, high = (slice(128 * h + i, 128 * h + j) for i, j in ((0, 128), (0, 64), (64, 128)))
                own = full.at[m, part, :]
                hops = [(own, up), (own, down), (full.at[self.mine(1), low, :], up), (full.at[self.mine(3), high, :], down)]
                self.z.append([remote(src, src, z_send.at[h, i], z_recv.at[h, i], to) for i, (src, to) in enumerate(hops)])
                slabs = [full.at[self.mine(k), part, :] for k in range(4)]
                self.b.append([remote(slabs[k], slabs[k], b_send.at[h, k], b_recv.at[h, k], at.sibling()) for k in range(4)])

        def mine(self, k):
            return ((z + 4 - k) % 4) * 2 + c

        def others(self, k):
            return ((z + 4 - k) % 4) * 2 + 1 - c

        def start(self):
            for h in (0, 1):
                self.z[h][0].start()
                self.z[h][1].start()
                self.b[h][0].start()

        def near(self, h):
            for i in (0, 1):
                self.z[h][i].wait_recv()
                self.z[h][2 + i].start()
                self.b[h][1 + 2 * i].start()

        def far(self, h):
            self.z[h][2].wait_recv()
            self.z[h][3].wait_recv()
            self.b[h][2].start()

        def other(self, k, h):
            self.b[h][k].wait_recv()

        def finish(self):
            for copy in self.z[0] + self.z[1] + self.b[0] + self.b[1]:
                copy.wait_send()

    mine = pl.ds(pl.multiple_of(a * rows, rows), rows)

    def spread_slab(full, s, half_of, buf, send, recv, near):
        lines = pl.ds(pl.multiple_of(a * rows + 128 * half_of, 128), 128)
        for h in (0, 1):
            bx, by = (2 * s + h) // 4, (2 * s + h) % 4
            q, j = bx * (1 - c) + by * c, bx * c + by * (1 - c)
            k = (q - a + 4) % 4
            n = (k + 3) % 4
            src = full.at[s, 128 * half_of : 128 * half_of + 128, pl.ds(h * half, half)]
            dst = buf.at[lines, pl.ds(pl.multiple_of(j * half, half), half)]

            @pl.when(k == 0)
            def _():
                pltpu.make_async_copy(src, dst, near.at[half_of, j]).start()

            @pl.when(k != 0)
            def _():
                remote(src, dst, send.at[half_of, n, j], recv.at[half_of, n, j], at.along_a(k)).start()

    def spread_ends(full, buf, send, recv, near):
        src, dst = full.at[0, 0:128, 0:half], buf.at[0:128, 0:half]
        far = [
            remote(src, dst, send.at[h, k - 1, j], recv.at[h, k - 1, j], at.along_a(k))
            for h in (0, 1)
            for k in (1, 2, 3)
            for j in range(4)
        ]
        local = [pltpu.make_async_copy(src, dst, near.at[h, j]) for h in (0, 1) for j in range(4)]
        return far, local

    def shard_rows(s):
        return pl.ds(pl.multiple_of(s * width, width), width)

    cots = Collect(cot_full, cz, czr, cb, cbr)
    cots.start()
    load_wo.wait()

    def add_heads(s, first=False):
        term = jnp.dot(cot_full[s], wo[shard_rows(s), :], preferred_element_type=F32)
        d_heads[...] = term if first else d_heads[...] + term

    def spread_cot(s, h):
        spread_slab(cot_full, s, h, cot_a, cs, cr, cl)

    add_heads(m, True)
    cots.near(0)
    cots.other(0, 0)
    cots.other(0, 1)
    add_heads(cots.others(0))
    cots.near(1)
    add_heads(cots.mine(1))
    add_heads(cots.mine(3))

    for copy in routes:
        copy.wait()
    arrived = inbox[:, width : width + 1].astype(F32)
    put = (lax.broadcasted_iota(jnp.int32, (512, rows), 1).astype(F32) + 1.0 == arrived).astype(BF16)
    block = tn_dot(put, inbox[:, 0:width])
    packed[...] = block.astype(BF16)

    def exchange(first, second, out, into, send, recv):
        lane = lax.broadcasted_iota(jnp.int32, (rows, 128), 1)
        out[...] = jnp.where(lane == 0, first, jnp.where(lane == 1, second, 0.0)).T[0:8]
        return [remote(out, into.at[k - 1], send.at[k - 1], recv.at[k - 1], at.along_m(k)) for k in range(1, 8)]

    part_mean = jnp.mean(block, -1, keepdims=True)
    part_center = block - part_mean
    stats = exchange(part_mean, jnp.sum(part_center * part_center, -1, keepdims=True), st_out, st_in, sts, str_)
    for copy in stats:
        copy.start()

    for h in (0, 1):
        spread_cot(m, h)
        spread_cot(cots.others(0), h)
        for k in (1, 3):
            spread_cot(cots.mine(k), h)
            cots.other(k, h)
            spread_cot(cots.others(k), h)
    cots.far(0)
    spread_cot(cots.mine(2), 0)
    for copy in stats:
        copy.wait()
    parts = [st_out[...]] + [st_in[k] for k in range(7)]
    mean = sum(part[0:1] for part in parts) * 0.125
    spread = sum(part[1:2] + width * (part[0:1] - mean) * (part[0:1] - mean) for part in parts)
    st_pad[0:1, :] = mean
    st_pad[1:2, :] = lax.rsqrt(spread * (1.0 / 6144.0) + 1e-06)
    columns[...] = st_pad[...].T
    gain_part = gain[:, pl.ds(pl.multiple_of(m * width, width), width)]
    unit = (packed[...].astype(F32) - columns[:, 0:1]) * columns[:, 1:2]
    normed_full[m] = (unit * gain_part).astype(BF16)
    norms = Collect(normed_full, nz, nzr, nb, nbr)
    norms.start()

    def spread_normed(s, h):
        spread_slab(normed_full, s, h, normed_a, ns, nr, nl)

    def add_projected(s, first=False):
        for t in range(3):
            cols = slice(t * half, (t + 1) * half)
            term = jnp.dot(normed_full[s], wq[t, shard_rows(s), :], preferred_element_type=F32)
            proj[:, cols] = term if first else proj[:, cols] + term

    cots.far(1)
    spread_cot(cots.mine(2), 1)
    for h in (0, 1):
        cots.other(2, h)
        spread_cot(cots.others(2), h)
    for h in (0, 1):
        spread_normed(m, h)
    norms.near(0)
    for k in (1, 3):
        spread_normed(norms.mine(k), 0)
    for h in (0, 1):
        norms.other(0, h)
        spread_normed(norms.others(0), h)
    load_wq.wait()
    add_projected(m, True)
    add_projected(norms.others(0))
    for k in (1, 3):
        norms.other(k, 0)
        spread_normed(norms.others(k), 0)
    for s in (cots.others(1), cots.others(3), cots.mine(2), cots.others(2)):
        add_heads(s)
    norms.near(1)
    norms.far(0)
    spread_normed(norms.mine(2), 0)
    for k in (1, 3):
        spread_normed(norms.mine(k), 1)
        add_projected(norms.mine(k))
    norms.other(2, 0)
    spread_normed(norms.others(2), 0)
    for k in (1, 3):
        norms.other(k, 1)
        spread_normed(norms.others(k), 1)
    for k in (1, 3):
        add_projected(norms.others(k))
    norms.far(1)
    spread_normed(norms.mine(2), 1)
    norms.other(2, 1)
    spread_normed(norms.others(2), 1)
    add_projected(norms.mine(2))
    add_projected(norms.others(2))
    same = places[:, 1:2] == segment[...].astype(F32)

    def normalise(values):
        center = values - jnp.mean(values, -1, keepdims=True)
        inverse = lax.rsqrt(jnp.mean(center * center, -1, keepdims=True) + 1e-06)
        return center * inverse, inverse

    def normalise_back(grad, unit, inverse, weight):
        scaled = grad.astype(BF16).astype(F32) * weight
        inner = scaled - jnp.mean(scaled, -1, keepdims=True) - unit * jnp.mean(scaled * unit, -1, keepdims=True)
        return (inverse * inner).astype(BF16)

    root = DH ** (-0.5)
    for h in range(3):
        q_cols, k_cols, v_cols = (slice(t * half + h * DH, t * half + (h + 1) * DH) for t in range(3))
        h_cols = slice(h * DH, (h + 1) * DH)
        unit_q, inverse_q = normalise(proj[:, q_cols])
        unit_k, inverse_k = normalise(proj[:, k_cols])
        queries = (unit_q * qk_gain[0:1, :]).astype(BF16)
        keys = (unit_k * qk_gain[1:2, :]).astype(BF16)
        values = proj[:, v_cols].astype(BF16)
        raised = jnp.where(same, jnp.exp(nt_dot(queries, keys) * root), 0.0)
        exact = raised / jnp.sum(raised, -1, keepdims=True)
        weights = exact.astype(BF16)
        heads[:, h_cols] = jnp.dot(weights, values, preferred_element_type=F32).astype(BF16)
        given = d_heads[:, h_cols].astype(BF16)
        d_weights = nt_dot(given, values).astype(BF16).astype(F32)
        dproj[:, v_cols] = tn_dot(weights, given).astype(BF16)
        inner = jnp.sum(d_weights * exact, -1, keepdims=True)
        d_scores = (exact * (d_weights - inner) * root).astype(BF16)
        d_queries = jnp.dot(d_scores, keys, preferred_element_type=F32)
        d_keys = tn_dot(d_scores, queries)
        dproj[:, q_cols] = normalise_back(d_queries, unit_q, inverse_q, qk_gain[0:1, :])
        dproj[:, k_cols] = normalise_back(d_keys, unit_k, inverse_k, qk_gain[1:2, :])

    for part in range(4):
        block = heads[...] if part == 0 else dproj[:, (part - 1) * half : part * half]
        parts_a[part, :, mine] = block.T

    def window(part, k, lines):
        cols = pl.ds(pl.multiple_of(((a + k) % 4) * rows, rows), rows)
        return parts_a.at[part, lines, cols]

    low, high, every = slice(0, 192), slice(192, 384), slice(0, 384)
    gathers = []
    for part in range(4):
        hops = [(0, every, 1), (0, every, 3), (0, every, 2)]
        refs = [(window(part, k, lines), at.along_a(to)) for k, lines, to in hops]
        gathers.append([remote(src, src, gs.at[part, i], gr.at[part, i], to) for i, (src, to) in enumerate(refs)])
    for part in range(4):
        gathers[part][0].start()
        gathers[part][1].start()
        gathers[part][2].start()

    def gathered(part):
        for copy in gathers[part]:
            copy.wait_recv()

    def held(part, i):
        return slice((3 * part + i) * half, (3 * part + i + 1) * half)

    def product(part, k):
        left = cot_a if part == 0 else normed_a
        cols = pl.ds(pl.multiple_of(((b + k) % 4) * half, half), half)
        return jnp.dot(parts_a[part], left[:, cols], preferred_element_type=F32)

    sums = []
    for part in range(4):
        out = [wo.at[held(part, i), :] for i in range(3)]
        sums.append(
            Ring(
                functools.partial(product, part), out, own_part.at[part], far_in.at[part], near_in.at[part],
                qs.at[part], qr.at[part], at.along_b,
            )
        )

    cot_far, cot_near = spread_ends(cot_full, cot_a, cs, cr, cl)

    def attn_term(shard):
        return jnp.dot(wo[shard_rows(shard), :], parts_a[0, :, mine], preferred_element_type=F32)

    def dn_term(shard):
        rows_of = shard_rows(shard)
        terms = (jnp.dot(wq[t, rows_of, :], parts_a[t + 1, :, mine], preferred_element_type=F32) for t in range(3))
        return sum(terms)

    class ChipSum:
        def __init__(self, term, out, into, send, recv):
            self.term, self.out, self.into = term, out, into
            self.copies = [remote(out.at[k], into.at[k], send.at[k], recv.at[k], at.sibling()) for k in range(4)]

        def start(self):
            for k in (2, 1, 3, 0):
                self.out[k] = self.term(((z + k) % 4) * 2 + 1 - c).astype(BF16)
                self.copies[k].start()

        def sum(self, k):
            value = self.term(((z + k) % 4) * 2 + c)
            self.copies[k].wait()
            return value + self.into[k].astype(F32)

    attn_chip = ChipSum(attn_term, sib_out, sib_in, ss, sr)
    dn_chip = ChipSum(dn_term, dn_sib_out, dn_sib_in, dss, dsr)
    attn_out = [z_out.at[i] for i in range(3)]
    dn_out = [dn_z_out.at[i] for i in range(3)]
    attn_ring = Ring(attn_chip.sum, attn_out, own_at, z_in.at[0], z_in.at[1:3], zs, zr, at.along_z)
    dn_ring = Ring(dn_chip.sum, dn_out, own_dn, dn_z_in.at[0], dn_z_in.at[1:3], dzs, dzr, at.along_z)

    attn_chip.start()
    dn_chip.start()
    attn_ring.send_far()
    dn_ring.send_far()
    attn_ring.send_near()
    dn_ring.send_near()
    cots.finish()
    for copy in cot_far + cot_near:
        copy.wait()
    gathered(0)
    sums[0].send_far()
    norms.finish()
    normed_far, normed_near = spread_ends(normed_full, normed_a, ns, nr, nl)
    for copy in normed_far + normed_near:
        copy.wait()
    sums[0].send_near()
    for part in (1, 2, 3):
        gathered(part)
        sums[part].send_far()
    sums[1].send_near()
    sums[2].send_near()
    sums[3].send_near()

    stores = [pltpu.make_async_copy(output, output_to, osem.at[0]), pltpu.make_async_copy(input_grad, input_grad_to, osem.at[1])]
    stores.append(pltpu.make_async_copy(out_grad, out_grad_to, osem.at[2]))
    stores += [pltpu.make_async_copy(qkv_grad.at[t], qkv_grad_to.at[t], osem.at[3 + t]) for t in range(3)]
    output[...] = (packed[...].astype(F32) + attn_ring.total().T).astype(BF16)
    stores[0].start()
    total = dn_ring.total().T
    rstd = columns[:, 1:2]
    unit = (packed[...].astype(F32) - columns[:, 0:1]) * rstd
    u = total * gain_part
    proj[:, 0:width] = u
    ends = exchange(jnp.sum(u, -1, keepdims=True), jnp.sum(u * unit, -1, keepdims=True), en_out, en_in, ens, enr)
    for copy in ends:
        copy.start()
    for copy in ends:
        copy.wait()
    st_pad[0:8, :] = (en_out[...] + sum(en_in[k] for k in range(7))) * (1.0 / 6144.0)
    means = st_pad[...].T
    unit = (packed[...].astype(F32) - columns[:, 0:1]) * rstd
    grad = rstd * (proj[:, 0:width] - means[:, 0:1] - unit * means[:, 1:2])
    input_grad[...] = (cot[...].astype(F32) + grad).astype(BF16)
    stores[1].start()
    for part in range(4):
        result = (sums[part].total() * scale).T.astype(BF16)
        if part == 0:
            out_grad[...] = result
        else:
            qkv_grad[part - 1] = result
        stores[2 + part].start()
    for ring in sums + [attn_ring, dn_ring]:
        ring.finish()
    for part in range(4):
        for copy in gathers[part]:
            copy.wait_send()
    for copy in stores:
        copy.wait()


def hand_over(*refs):
    sources, results, held, came, went = refs[:4], refs[4:8], refs[8:12], refs[12], refs[13]
    ins = [pltpu.make_async_copy(src, buf, came.at[i]) for i, (src, buf) in enumerate(zip(sources, held))]
    outs = [pltpu.make_async_copy(buf, dst, went.at[i]) for i, (buf, dst) in enumerate(zip(held, results))]
    for copy in ins:
        copy.start()
    for before, after in zip(ins, outs):
        before.wait()
        after.start()
    for copy in outs:
        copy.wait()


def shards(patches, dest_group, dest_row, segment, ln_gain, w_qkv, qk_gain, w_out, cotangent):
    anywhere = pl.BlockSpec(memory_space=pl.ANY)
    dma = pltpu.SemaphoreType.DMA
    V = pltpu.VMEM
    scale = 1.0 / math.sqrt(4096)
    out_shape = (
        jax.ShapeDtypeStruct((256, 768), BF16),
        jax.ShapeDtypeStruct((256, 768), BF16),
        jax.ShapeDtypeStruct((3, 384, 384), BF16),
        jax.ShapeDtypeStruct((384, 384), BF16),
    )
    results = pl.pallas_call(
        functools.partial(whole, scale),
        out_shape=out_shape,
        in_specs=[anywhere] * 9,
        out_specs=(anywhere,) * 4,
        scratch_shapes=[
            V((256, 768), BF16), V((1, 256), jnp.int32), V((1, 256), jnp.int32), V((1, 256), jnp.int32),
            V((1, 6144), F32), V((2, 128), F32), V((256, 768), BF16),
            *(V(shape.shape, BF16) for shape in out_shape),
            V((512, 896), BF16), V((512, 896), BF16), V((256, 768), BF16),
            V((8, 256, 768), BF16), V((8, 256, 768), BF16),
            V((1024, 1536), BF16), V((1024, 1536), BF16), V((4, 384, 1024), BF16),
            V((3, 6144, 384), BF16), V((6144, 384), BF16),
            V((256, 1152), F32), V((256, 384), F32), V((256, 384), BF16), V((256, 1152), BF16),
            V((256, 128), F32), V((256, 128), F32), V((128, 256), F32),
            V((8, 256), F32), V((7, 8, 256), F32), V((8, 256), F32), V((7, 8, 256), F32),
            V((4, 768, 256), BF16), V((4, 768, 256), BF16), V((3, 768, 256), BF16), V((3, 768, 256), BF16),
            V((4, 768, 256), BF16), V((4, 768, 256), BF16), V((3, 768, 256), BF16), V((3, 768, 256), BF16),
            V((4, 384, 384), BF16), V((4, 2, 384, 384), BF16),
            V((4, 384, 384), F32), V((768, 256), F32), V((768, 256), F32),
            dma((8,)), dma((6,)), dma((2,)), dma((15,)), dma((15,)),
            dma((2, 4)), dma((2, 4)), dma((2, 4)), dma((2, 4)), dma((2, 4)), dma((2, 4)), dma((2, 4)), dma((2, 4)),
            dma((7,)), dma((7,)), dma((7,)), dma((7,)),
            dma((2, 3, 4)), dma((2, 3, 4)), dma((2, 4)), dma((2, 3, 4)), dma((2, 3, 4)), dma((2, 4)),
            dma((4, 4)), dma((4, 4)),
            dma((4,)), dma((4,)), dma((4,)), dma((4,)), dma((4,)), dma((4,)), dma((4,)), dma((4,)),
            dma((4, 4)), dma((4, 4)),
        ],
        compiler_params=pltpu.CompilerParams(
            collective_id=1, has_side_effects=True, vmem_limit_bytes=62 << 20
        ),
        name="whole",
    )(
        patches, dest_group.reshape(1, 256), dest_row.reshape(1, 256), segment.reshape(1, 256),
        ln_gain.reshape(1, 6144), jnp.transpose(w_qkv, (1, 0, 2)), qk_gain, w_out, cotangent,
    )
    output, input_grad, qkv_grad, out_grad = pl.pallas_call(
        hand_over,
        out_shape=out_shape,
        in_specs=[anywhere] * 4,
        out_specs=(anywhere,) * 4,
        scratch_shapes=[V(shape.shape, BF16) for shape in out_shape] + [dma((4,)), dma((4,))],
        name="hand_over",
    )(*results)
    return (output, input_grad, jnp.transpose(qkv_grad, (1, 0, 2)), out_grad)


def solution(mesh):
    placed = (
        P("dp", "mp"),
        P("dp"),
        P("dp"),
        P("dp"),
        P(),
        P(None, None, "mp"),
        P(),
        P(None, "mp"),
        P("dp", "mp"),
    )
    return jax.shard_map(
        shards,
        mesh=mesh,
        in_specs=placed,
        out_specs=(P("dp", "mp"), P("dp", "mp"), P("dp", None, "mp"), P("dp", "mp")),
        check_vma=False,
    )
```
